128 devices in a mesh: section: 8 (over z_hi, x), dp: 16 (over z_lo, y, core).
Axes of the slice: x: 4, y: 4, z: 4 (z_hi: 2, z_lo: 2; z = z_hi * 2 + z_lo), core: 2. Of those that a mesh axis runs over, the one named last changes fastest.
Arguments:
- clean: bfloat16 [64, 16, 16, 384], P('dp'), may hold values from -12 to 12
- noise: bfloat16 [64, 16, 16, 384], P('dp'), may hold values from -6 to 6
- stamps: int32 [64], P('dp'), may hold values from 0 to 999
- enc_weight: bfloat16 [8, 3, 3, 384, 384], P('section'), may hold values from -0.109375 to 0.109375
- dec_weight: bfloat16 [8, 3, 3, 768, 384], P('section'), may hold values from -0.078125 to 0.078125
Outputs:
- enc_grad: float32 [8, 3, 3, 384, 384], P('section', None, None, 'dp')
- dec_grad: float32 [8, 3, 3, 768, 384], P('section', None, None, 'dp')
The draws below stay inside these ranges and needn't reach their ends.
All inputs are finite; a program needn't handle non-finite values.
Results may differ from the reference program's by a relative error of at most 0.0035.
Values sent between devices are 32-bit elements; how exact they have to be, the bound alone decides.
A program may use at most 128 MiB of HBM per device.

```python
import math
import jax
import jax.numpy as jnp
from jax import lax

C = 384
GROUPS = 32
RES = 16
BATCH = 64
N_SECTION = 8


def draw_clean(key, part):
    base_key, scale_key = jax.random.split(key)
    scales = 0.3 * jnp.exp(jax.random.uniform(scale_key, (BATCH, 1, 1, C), jnp.float32, 0.0, math.log(10.0)))
    base_values = jnp.clip(jax.random.normal(base_key, (BATCH, RES, RES, C), jnp.float32), -4.0, 4.0)
    return (base_values * scales).astype(jnp.bfloat16)


def place_ends(result, key, smallest, largest):
    place = [jax.random.randint(jax.random.fold_in(key, axis), (), 0, length) for axis, length in enumerate(result.shape)]
    longest = result.shape.index(max(result.shape))
    next_to = place[:longest] + [(place[longest] + 1) % result.shape[longest]] + place[longest + 1:]
    return result.at[tuple(place)].set(smallest).at[tuple(next_to)].set(largest)


def block_scale(stream_key, dims, cuts, smallest, high):
    def one(position, parts):
        heights = jax.random.uniform(jax.random.fold_in(jax.random.fold_in(stream_key, 6), position), (parts,), jnp.float32, smallest / len(cuts), high / len(cuts))
        return jnp.repeat(jnp.exp(heights), dims[position] // parts).reshape((-1,) + (1,) * (len(dims) - position - 1))

    loudness = one(*cuts[0])
    for cut in cuts[1:]:
        loudness = loudness * one(*cut)
    return loudness


def bell_draw(own_key, shape, spread, reach, pieces=(), kind=jnp.bfloat16):
    array = spread * jax.random.normal(own_key, shape, jnp.float32)
    if pieces:
        array = array * block_scale(own_key, shape, pieces, -0.22, 0.18)
    return jnp.clip(array, -reach, reach).astype(kind)


def setup_inputs(seed: int = 0) -> dict:
    key_list = jax.random.split(jax.random.key(seed), 6)
    return {
        "clean": draw_clean(jax.random.fold_in(key_list[5], 71), 0),
        "noise": bell_draw(key_list[1], (BATCH, RES, RES, C), 1.0, 6.0, ((0, 16),)),
        "stamps": place_ends(jax.random.randint(key_list[2], (BATCH,), 0, 1000), jax.random.fold_in(key_list[2], 1), 0, 999).astype(jnp.int32),
        "enc_weight": bell_draw(key_list[3], (N_SECTION, 3, 3, C, C), (9 * C) ** -0.5, 0.109375, ((0, 8),)),
        "dec_weight": bell_draw(key_list[4], (N_SECTION, 3, 3, 2 * C, C), (18 * C) ** -0.5, 0.078125, ((0, 8),)),
    }


def embed(stamps_in, channels):
    half_width = channels // 2
    frequency = jnp.exp(-math.log(10000.0) * jnp.arange(half_width, dtype=jnp.float32) / half_width)
    angles = stamps_in.astype(jnp.float32)[:, None] * frequency[None, :]
    return jnp.concatenate([jnp.sin(angles), jnp.cos(angles)], axis=1)

def activate(inputs_f32, stamps_in):
    batch_rows, height, breadth, channels = inputs_f32.shape
    grouped = inputs_f32.reshape(batch_rows, height * breadth, GROUPS, channels // GROUPS)
    group_mean = lax.optimization_barrier(jnp.mean(grouped, axis=(1, 3), keepdims=True))
    centered = grouped - group_mean
    group_var = lax.optimization_barrier(jnp.mean(centered * centered, axis=(1, 3), keepdims=True))
    normed = (centered * lax.rsqrt(group_var + 1e-05)).reshape(inputs_f32.shape)
    modulate = 1.0 + 0.5 * embed(stamps_in, channels)[:, None, None, :]
    return jax.nn.silu(normed * modulate)

def conv_apply(activations, weight):
    batch_rows, height, breadth, channels = activations.shape
    padded = jnp.pad(activations, ((0, 0), (1, 1), (1, 1), (0, 0)))
    summed = jnp.zeros((batch_rows * height * breadth, weight.shape[3]), jnp.float32)
    for row_off in range(3):
        for col_off in range(3):
            window = padded[:, row_off:row_off + height, col_off:col_off + breadth, :].reshape(-1, channels)
            summed = summed + jnp.dot(window, weight[row_off, col_off], preferred_element_type=jnp.float32)
    return summed.reshape(batch_rows, height, breadth, weight.shape[3])

def conv_back(cotangent, weight):
    batch_rows, height, breadth, outputs = cotangent.shape
    padded = jnp.pad(cotangent.astype(jnp.bfloat16), ((0, 0), (1, 1), (1, 1), (0, 0)))
    summed = jnp.zeros((batch_rows * height * breadth, weight.shape[2]), jnp.float32)
    for row_off in range(3):
        for col_off in range(3):
            window = padded[:, 2 - row_off:2 - row_off + height, 2 - col_off:2 - col_off + breadth, :].reshape(-1, outputs)
            summed = summed + lax.dot_general(window, weight[row_off, col_off], (((1,), (1,)), ((), ())), preferred_element_type=jnp.float32)
    return summed.reshape(batch_rows, height, breadth, weight.shape[2])

def conv_weight_grad(activations, cotangent):
    batch_rows, height, breadth, channels = activations.shape
    padded = jnp.pad(activations, ((0, 0), (1, 1), (1, 1), (0, 0)))
    flat_cot = cotangent.astype(jnp.bfloat16).reshape(-1, cotangent.shape[3])
    kernel_rows = []
    for row_off in range(3):
        kernel_cols = []
        for col_off in range(3):
            window = padded[:, row_off:row_off + height, col_off:col_off + breadth, :].reshape(-1, channels)
            kernel_cols.append(lax.dot_general(window, flat_cot, (((0,), (0,)), ((), ())), preferred_element_type=jnp.float32))
        kernel_rows.append(jnp.stack(kernel_cols))
    return jnp.stack(kernel_rows)

def block_forward(inputs, residual, weight, stamps_in):
    activations = activate(inputs.astype(jnp.float32), stamps_in).astype(jnp.bfloat16)
    return residual.astype(jnp.float32) + conv_apply(activations, weight)

def block_backward(inputs, weight, stamps_in, cotangent):
    activated, pullback = jax.vjp(lambda inner_field: activate(inner_field, stamps_in), inputs.astype(jnp.float32))
    activations = activated.astype(jnp.bfloat16)
    weight_grad = conv_weight_grad(activations, cotangent)
    input_grad = pullback(conv_back(cotangent, weight))[0]
    return (input_grad, weight_grad)

def noise_levels(stamps_in):
    phase = (stamps_in.astype(jnp.float32) / 1000.0 + 0.008) / 1.008 * (math.pi / 2.0)
    signal = jnp.cos(phase) ** 2
    return (jnp.sqrt(signal), jnp.sqrt(1.0 - signal))

def reference(clean, noise, stamps, enc_weight, dec_weight):
    keep_level, spread_level = noise_levels(stamps)
    state_now = keep_level[:, None, None, None] * clean.astype(jnp.float32) + spread_level[:, None, None, None] * noise.astype(jnp.float32)
    enc_inputs = []
    skips = []
    for block_id in range(N_SECTION):
        enc_inputs.append(state_now)
        state_now = block_forward(state_now, state_now, enc_weight[block_id], stamps)
        skips.append(state_now)
    dec_inputs = [state_now] * N_SECTION
    for block_id in reversed(range(N_SECTION)):
        dec_inputs[block_id] = state_now
        joined = jnp.concatenate([state_now, skips[block_id]], axis=3)
        state_now = block_forward(joined, state_now, dec_weight[block_id], stamps)
    factor = 1.0 / math.sqrt(BATCH * RES * RES)
    flowing = factor * (state_now - noise.astype(jnp.float32))
    dec_grads = []
    skip_grads = []
    for block_id in range(N_SECTION):
        joined = jnp.concatenate([dec_inputs[block_id], skips[block_id]], axis=3)
        input_grad, weight_grad = block_backward(joined, dec_weight[block_id], stamps, flowing)
        dec_grads.append(weight_grad)
        skip_grads.append(input_grad[..., C:])
        flowing = input_grad[..., :C] + flowing
    enc_grads = [dec_grads[0]] * N_SECTION
    for block_id in reversed(range(N_SECTION)):
        merged = flowing + skip_grads[block_id]
        input_grad, weight_grad = block_backward(enc_inputs[block_id], enc_weight[block_id], stamps, merged)
        enc_grads[block_id] = weight_grad
        flowing = input_grad + merged
    return (jnp.stack(enc_grads), jnp.stack(dec_grads))
```

```python
import math

import jax
import jax.numpy as jnp
from jax import lax
from jax.sharding import PartitionSpec as P

GROUPS = 32


def passed_along(value, axis, steps):
    count = lax.axis_size(axis)
    initial, last = (max(0, -steps), min(count, count - steps))
    return lax.ppermute(value, axis, [(source, source + steps) for source in range(initial, last)])


def embed(stamps_in, channels):
    half_width = channels // 2
    frequency = jnp.exp(-math.log(10000.0) * jnp.arange(half_width, dtype=jnp.float32) / half_width)
    angles = stamps_in.astype(jnp.float32)[:, None] * frequency[None, :]
    return jnp.concatenate([jnp.sin(angles), jnp.cos(angles)], axis=1)


def activate(inputs_f32, stamps_in):
    batch_rows, height, breadth, channels = inputs_f32.shape
    grouped = inputs_f32.reshape(batch_rows, height * breadth, GROUPS, channels // GROUPS)
    group_mean = jnp.mean(grouped, axis=(1, 3), keepdims=True)
    centered = grouped - group_mean
    group_var = jnp.mean(centered * centered, axis=(1, 3), keepdims=True)
    normed = (centered * lax.rsqrt(group_var + 1e-05)).reshape(inputs_f32.shape)
    modulate = 1.0 + 0.5 * embed(stamps_in, channels)[:, None, None, :]
    return jax.nn.silu(normed * modulate)


def conv_apply(activations, weight):
    batch_rows, height, breadth, channels = activations.shape
    padded = jnp.pad(activations, ((0, 0), (1, 1), (1, 1), (0, 0)))
    summed = jnp.zeros((batch_rows * height * breadth, weight.shape[3]), jnp.float32)
    for row_off in range(3):
        for col_off in range(3):
            window = padded[:, row_off : row_off + height, col_off : col_off + breadth, :].reshape(
                -1, channels
            )
            summed = summed + jnp.dot(
                window, weight[row_off, col_off], preferred_element_type=jnp.float32
            )
    return summed.reshape(batch_rows, height, breadth, weight.shape[3])


def conv_back(cotangent, weight):
    batch_rows, height, breadth, outputs = cotangent.shape
    padded = jnp.pad(cotangent.astype(jnp.bfloat16), ((0, 0), (1, 1), (1, 1), (0, 0)))
    summed = jnp.zeros((batch_rows * height * breadth, weight.shape[2]), jnp.float32)
    for row_off in range(3):
        for col_off in range(3):
            window = padded[
                :, 2 - row_off : 2 - row_off + height, 2 - col_off : 2 - col_off + breadth, :
            ].reshape(-1, outputs)
            summed = summed + lax.dot_general(
                window,
                weight[row_off, col_off],
                (((1,), (1,)), ((), ())),
                preferred_element_type=jnp.float32,
            )
    return summed.reshape(batch_rows, height, breadth, weight.shape[2])


def conv_weight_grad(activations, cotangent):
    batch_rows, height, breadth, channels = activations.shape
    padded = jnp.pad(activations, ((0, 0), (1, 1), (1, 1), (0, 0)))
    flat_cot = cotangent.astype(jnp.bfloat16).reshape(-1, cotangent.shape[3])
    kernel_rows = []
    for row_off in range(3):
        kernel_cols = []
        for col_off in range(3):
            window = padded[:, row_off : row_off + height, col_off : col_off + breadth, :].reshape(
                -1, channels
            )
            kernel_cols.append(
                lax.dot_general(
                    window, flat_cot, (((0,), (0,)), ((), ())), preferred_element_type=jnp.float32
                )
            )
        kernel_rows.append(jnp.stack(kernel_cols))
    return jnp.stack(kernel_rows)


def block_forward(inputs, residual, weight, stamps_in):
    activations = activate(inputs, stamps_in).astype(jnp.bfloat16)
    return residual + conv_apply(activations, weight)


def block_backward(inputs, weight, stamps_in, cotangent):
    activated, pullback = jax.vjp(lambda inner_field: activate(inner_field, stamps_in), inputs)
    activations = activated.astype(jnp.bfloat16)
    weight_grad = conv_weight_grad(activations, cotangent)
    input_grad = pullback(conv_back(cotangent, weight))[0]
    return (input_grad, weight_grad)


def noise_levels(stamps_in):
    phase = (stamps_in.astype(jnp.float32) / 1000.0 + 0.008) / 1.008 * (math.pi / 2.0)
    signal = jnp.cos(phase) ** 2
    return (jnp.sqrt(signal), jnp.sqrt(1.0 - signal))


def pick_row(buffer, slot_index):
    return lax.dynamic_slice_in_dim(buffer, slot_index, 1, 0)


def put_row(buffer, piece, slot_index):
    return lax.dynamic_update_slice_in_dim(buffer, piece, slot_index, 0)


def shards(clean, noise, stamps, enc_weight, dec_weight):
    sections = lax.axis_size("section")
    section_index = lax.axis_index("section")
    last_section = sections - 1
    samples = clean.shape[0]
    channels = clean.shape[3]
    enc_kernel = enc_weight[0]
    dec_kernel = dec_weight[0]
    keep_level, spread_level = noise_levels(stamps)
    noisy = keep_level[:, None, None, None] * clean.astype(jnp.float32) + spread_level[
        :, None, None, None
    ] * noise.astype(jnp.float32)
    factor = 1.0 / math.sqrt(samples * lax.axis_size("dp") * clean.shape[1] * clean.shape[2])
    blank_piece = jnp.zeros((1,) + clean.shape[1:], jnp.float32)
    blank_buffer = jnp.zeros((samples + 2,) + clean.shape[1:], jnp.float32)

    enc_fwd_off = section_index
    dec_fwd_off = 2 * sections - 1 - section_index
    dec_back_off = 2 * sections + section_index
    enc_back_off = 4 * sections - 1 - section_index

    def locate(tick_now, offset):
        sample_id = tick_now - offset
        active = (sample_id >= 0) & (sample_id < samples)
        clipped = jnp.clip(sample_id, 0, samples - 1)
        slot_index = jnp.clip(sample_id, -1, samples) + 1
        return (active, clipped, slot_index)

    def make_tick(tasks):
        def tick(tick_now, carried):
            (fwd_in, bwd_in, enc_inputs, skips, dec_inputs, outputs, skip_grads, up_grads,
             enc_acc, dec_acc) = carried
            fwd_out = blank_piece
            bwd_out = blank_piece
            if "enc_fwd" in tasks:
                active, sample_at, slot_index = locate(tick_now, enc_fwd_off)
                source = jnp.where(section_index == 0, pick_row(noisy, sample_at), fwd_in)
                stamp_one = pick_row(stamps, sample_at)
                result = lax.cond(
                    active,
                    lambda: block_forward(source, source, enc_kernel, stamp_one),
                    lambda: blank_piece,
                )
                enc_inputs = put_row(enc_inputs, source, slot_index)
                skips = put_row(skips, result, slot_index)
                fwd_out = jnp.where(active, result, fwd_out)
            if "dec_fwd" in tasks:
                active, sample_at, slot_index = locate(tick_now, dec_fwd_off)
                skip_piece = pick_row(skips, slot_index)
                source = jnp.where(section_index == last_section, skip_piece, bwd_in)
                joined = jnp.concatenate([source, skip_piece], axis=3)
                stamp_one = pick_row(stamps, sample_at)
                result = lax.cond(
                    active,
                    lambda: block_forward(joined, source, dec_kernel, stamp_one),
                    lambda: blank_piece,
                )
                dec_inputs = put_row(dec_inputs, source, slot_index)
                outputs = put_row(outputs, result, slot_index)
                bwd_out = jnp.where(active, result, bwd_out)
            if "dec_back" in tasks:
                active, sample_at, slot_index = locate(tick_now, dec_back_off)
                top_grad = factor * (
                    pick_row(outputs, slot_index) - pick_row(noise, sample_at).astype(jnp.float32)
                )
                flowing = jnp.where(section_index == 0, top_grad, fwd_in)
                joined = jnp.concatenate(
                    [pick_row(dec_inputs, slot_index), pick_row(skips, slot_index)], axis=3
                )
                stamp_one = pick_row(stamps, sample_at)

                def decoder_working(accum):
                    input_grad, weight_grad = block_backward(joined, dec_kernel, stamp_one, flowing)
                    up_piece = input_grad[..., :channels] + flowing
                    return (accum + weight_grad, up_piece, input_grad[..., channels:])

                def decoder_resting(accum):
                    return (accum, blank_piece, blank_piece)

                dec_acc, up_piece, skip_grad = lax.cond(
                    active, decoder_working, decoder_resting, dec_acc
                )
                skip_grads = put_row(skip_grads, skip_grad, slot_index)
                up_grads = put_row(up_grads, up_piece, slot_index)
                fwd_out = jnp.where(active, up_piece, fwd_out)
            if "enc_back" in tasks:
                active, sample_at, slot_index = locate(tick_now, enc_back_off)
                arriving = jnp.where(
                    section_index == last_section, pick_row(up_grads, slot_index), bwd_in
                )
                merged = arriving + pick_row(skip_grads, slot_index)
                block_input = pick_row(enc_inputs, slot_index)
                stamp_one = pick_row(stamps, sample_at)

                def encoder_working(accum):
                    input_grad, weight_grad = block_backward(
                        block_input, enc_kernel, stamp_one, merged
                    )
                    return (accum + weight_grad, input_grad + merged)

                def encoder_resting(accum):
                    return (accum, blank_piece)

                enc_acc, down_piece = lax.cond(active, encoder_working, encoder_resting, enc_acc)
                bwd_out = jnp.where(active, down_piece, bwd_out)
            if "enc_fwd" in tasks or "dec_back" in tasks:
                fwd_in = passed_along(fwd_out, "section", 1)
            if "dec_fwd" in tasks or "enc_back" in tasks:
                bwd_in = passed_along(bwd_out, "section", -1)
            return (fwd_in, bwd_in, enc_inputs, skips, dec_inputs, outputs, skip_grads, up_grads,
                    enc_acc, dec_acc)

        return tick

    dec_fwd_begin = sections
    dec_back_begin = 2 * sections
    enc_back_begin = 3 * sections
    dec_back_end = dec_back_begin + last_section + samples
    ticks_total = 4 * sections - 1 + samples
    stages = [
        (0, dec_fwd_begin, ("enc_fwd",)),
        (dec_fwd_begin, dec_back_begin, ("enc_fwd", "dec_fwd")),
        (dec_back_begin, enc_back_begin, ("dec_fwd", "dec_back")),
        (enc_back_begin, dec_back_end, ("dec_back", "enc_back")),
    ]
    carried = (
        blank_piece, blank_piece, blank_buffer, blank_buffer, blank_buffer, blank_buffer,
        blank_buffer, blank_buffer,
        jnp.zeros(enc_kernel.shape, jnp.float32), jnp.zeros(dec_kernel.shape, jnp.float32),
    )
    for begin, end, tasks in stages:
        carried = lax.fori_loop(begin, end, make_tick(tasks), carried)
    dec_acc = carried[9]
    dec_share = lax.psum_scatter(dec_acc[None], "dp", scatter_dimension=3, tiled=True)
    carried = lax.fori_loop(dec_back_end, ticks_total, make_tick(("enc_back",)), carried)
    enc_acc = carried[8]
    enc_share = lax.psum_scatter(enc_acc[None], "dp", scatter_dimension=3, tiled=True)
    return (enc_share, dec_share)


def solution(mesh):
    placed = (
        P("dp", None, None, None),
        P("dp", None, None, None),
        P("dp"),
        P("section", None, None, None, None),
        P("section", None, None, None, None),
    )
    return jax.shard_map(
        shards,
        mesh=mesh,
        in_specs=placed,
        out_specs=(P("section", None, None, "dp", None), P("section", None, None, "dp", None)),
        check_vma=False,
    )
```

```python
import math

import jax
import jax.numpy as jnp
from jax import lax
from jax.sharding import PartitionSpec as P

GROUPS = 32


def passed_along(value, axis, steps):
    count = lax.axis_size(axis)
    initial, last = (max(0, -steps), min(count, count - steps))
    return lax.ppermute(value, axis, [(source, source + steps) for source in range(initial, last)])


def embed(stamps_in, channels):
    half_width = channels // 2
    frequency = jnp.exp(-math.log(10000.0) * jnp.arange(half_width, dtype=jnp.float32) / half_width)
    angles = stamps_in.astype(jnp.float32)[:, None] * frequency[None, :]
    return jnp.concatenate([jnp.sin(angles), jnp.cos(angles)], axis=1)


def activate(inputs_f32, stamps_in):
    batch_rows, height, breadth, channels = inputs_f32.shape
    width = channels // GROUPS
    count = height * breadth * width

    def group_mean(values):
        per_channel = jnp.sum(values, axis=(1, 2))
        per_group = jnp.sum(per_channel.reshape(batch_rows, GROUPS, width), axis=2) / count
        return jnp.repeat(per_group, width, axis=1)[:, None, None, :]

    centered = inputs_f32 - group_mean(inputs_f32)
    group_var = group_mean(centered * centered)
    normed = centered * lax.rsqrt(group_var + 1e-05)
    modulate = 1.0 + 0.5 * embed(stamps_in, channels)[:, None, None, :]
    return jax.nn.silu(normed * modulate)


def conv_apply(activations, weight):
    batch_rows, height, breadth, channels = activations.shape
    padded = jnp.pad(activations, ((0, 0), (1, 1), (1, 1), (0, 0)))
    summed = jnp.zeros((batch_rows * height * breadth, weight.shape[3]), jnp.float32)
    for row_off in range(3):
        for col_off in range(3):
            window = padded[:, row_off : row_off + height, col_off : col_off + breadth, :].reshape(
                -1, channels
            )
            summed = summed + jnp.dot(
                window, weight[row_off, col_off], preferred_element_type=jnp.float32
            )
    return summed.reshape(batch_rows, height, breadth, weight.shape[3])


def conv_back(cotangent, weight):
    batch_rows, height, breadth, outputs = cotangent.shape
    padded = jnp.pad(cotangent.astype(jnp.bfloat16), ((0, 0), (1, 1), (1, 1), (0, 0)))
    summed = jnp.zeros((batch_rows * height * breadth, weight.shape[2]), jnp.float32)
    for row_off in range(3):
        for col_off in range(3):
            window = padded[
                :, 2 - row_off : 2 - row_off + height, 2 - col_off : 2 - col_off + breadth, :
            ].reshape(-1, outputs)
            summed = summed + lax.dot_general(
                window,
                weight[row_off, col_off],
                (((1,), (1,)), ((), ())),
                preferred_element_type=jnp.float32,
            )
    return summed.reshape(batch_rows, height, breadth, weight.shape[2])


def conv_weight_grad(activations, cotangent):
    batch_rows, height, breadth, channels = activations.shape
    padded = jnp.pad(activations, ((0, 0), (1, 1), (1, 1), (0, 0)))
    flat_cot = cotangent.astype(jnp.bfloat16).reshape(-1, cotangent.shape[3])
    kernel_rows = []
    for row_off in range(3):
        kernel_cols = []
        for col_off in range(3):
            window = padded[:, row_off : row_off + height, col_off : col_off + breadth, :].reshape(
                -1, channels
            )
            kernel_cols.append(
                lax.dot_general(
                    window, flat_cot, (((0,), (0,)), ((), ())), preferred_element_type=jnp.float32
                )
            )
        kernel_rows.append(jnp.stack(kernel_cols))
    return jnp.stack(kernel_rows)


def block_forward(inputs, residual, weight, stamps_in):
    activations = activate(inputs, stamps_in).astype(jnp.bfloat16)
    return residual + conv_apply(activations, weight)


def block_backward(inputs, weight, stamps_in, cotangent):
    activated, pullback = jax.vjp(lambda inner_field: activate(inner_field, stamps_in), inputs)
    activations = activated.astype(jnp.bfloat16)
    weight_grad = conv_weight_grad(activations, cotangent)
    input_grad = pullback(conv_back(cotangent, weight))[0]
    return (input_grad, weight_grad)


def noise_levels(stamps_in):
    phase = (stamps_in.astype(jnp.float32) / 1000.0 + 0.008) / 1.008 * (math.pi / 2.0)
    signal = jnp.cos(phase) ** 2
    return (jnp.sqrt(signal), jnp.sqrt(1.0 - signal))


def pick_row(buffer, slot_index):
    return lax.dynamic_slice_in_dim(buffer, slot_index, 1, 0)


def store_row(buffer, piece, slot_index, active):
    kept = pick_row(buffer, slot_index)
    return lax.dynamic_update_slice_in_dim(buffer, jnp.where(active, piece, kept), slot_index, 0)


def shards(clean, noise, stamps, enc_weight, dec_weight):
    sections = lax.axis_size("section")
    section_index = lax.axis_index("section")
    last_section = sections - 1
    samples = clean.shape[0]
    channels = clean.shape[3]
    enc_kernel = enc_weight[0]
    dec_kernel = dec_weight[0]
    keep_level, spread_level = noise_levels(stamps)
    noisy = keep_level[:, None, None, None] * clean.astype(jnp.float32) + spread_level[
        :, None, None, None
    ] * noise.astype(jnp.float32)
    factor = 1.0 / math.sqrt(samples * lax.axis_size("dp") * clean.shape[1] * clean.shape[2])
    ticks_total = samples + sections - 1
    blank_piece = jnp.zeros((1,) + clean.shape[1:], jnp.float32)
    blank_buffer = jnp.zeros(clean.shape, jnp.float32)

    def locate(tick_now, offset):
        sample_id = tick_now - offset
        active = (sample_id >= 0) & (sample_id < samples)
        slot_index = jnp.clip(sample_id, 0, samples - 1)
        return (active, slot_index)

    def encoder_tick(tick_now, carried):
        incoming, enc_inputs, skips = carried
        active, slot_index = locate(tick_now, section_index)
        source = jnp.where(section_index == 0, pick_row(noisy, slot_index), incoming)
        stamp_one = pick_row(stamps, slot_index)
        result = lax.cond(
            active,
            lambda: block_forward(source, source, enc_kernel, stamp_one),
            lambda: blank_piece,
        )
        enc_inputs = store_row(enc_inputs, source, slot_index, active)
        skips = store_row(skips, result, slot_index, active)
        incoming = passed_along(result, "section", 1)
        return (incoming, enc_inputs, skips)

    _, enc_inputs, skips = lax.fori_loop(
        0, ticks_total, encoder_tick, (blank_piece, blank_buffer, blank_buffer)
    )

    def decoder_tick(tick_now, carried):
        incoming, dec_inputs, outputs = carried
        active, slot_index = locate(tick_now, last_section - section_index)
        skip_piece = pick_row(skips, slot_index)
        source = jnp.where(section_index == last_section, skip_piece, incoming)
        joined = jnp.concatenate([source, skip_piece], axis=3)
        stamp_one = pick_row(stamps, slot_index)
        result = lax.cond(
            active,
            lambda: block_forward(joined, source, dec_kernel, stamp_one),
            lambda: blank_piece,
        )
        dec_inputs = store_row(dec_inputs, source, slot_index, active)
        outputs = store_row(outputs, result, slot_index, active)
        incoming = passed_along(result, "section", -1)
        return (incoming, dec_inputs, outputs)

    _, dec_inputs, outputs = lax.fori_loop(
        0, ticks_total, decoder_tick, (blank_piece, blank_buffer, blank_buffer)
    )

    def decoder_back_tick(tick_now, carried):
        incoming, dec_acc, skip_grads, up_grads = carried
        active, slot_index = locate(tick_now, section_index)
        top_grad = factor * (
            pick_row(outputs, slot_index) - pick_row(noise, slot_index).astype(jnp.float32)
        )
        flowing = jnp.where(section_index == 0, top_grad, incoming)
        joined = jnp.concatenate(
            [pick_row(dec_inputs, slot_index), pick_row(skips, slot_index)], axis=3
        )
        stamp_one = pick_row(stamps, slot_index)

        def decoder_working(accum):
            input_grad, weight_grad = block_backward(joined, dec_kernel, stamp_one, flowing)
            up_piece = input_grad[..., :channels] + flowing
            return (accum + weight_grad, up_piece, input_grad[..., channels:])

        def decoder_resting(accum):
            return (accum, blank_piece, blank_piece)

        dec_acc, up_piece, skip_grad = lax.cond(active, decoder_working, decoder_resting, dec_acc)
        skip_grads = store_row(skip_grads, skip_grad, slot_index, active)
        up_grads = store_row(up_grads, up_piece, slot_index, active)
        incoming = passed_along(up_piece, "section", 1)
        return (incoming, dec_acc, skip_grads, up_grads)

    dec_start = jnp.zeros(dec_kernel.shape, jnp.float32)
    _, dec_acc, skip_grads, up_grads = lax.fori_loop(
        0, ticks_total, decoder_back_tick, (blank_piece, dec_start, blank_buffer, blank_buffer)
    )

    def encoder_back_tick(tick_now, carried):
        incoming, enc_acc = carried
        active, slot_index = locate(tick_now, last_section - section_index)
        arriving = jnp.where(
            section_index == last_section, pick_row(up_grads, slot_index), incoming
        )
        merged = arriving + pick_row(skip_grads, slot_index)
        block_input = pick_row(enc_inputs, slot_index)
        stamp_one = pick_row(stamps, slot_index)

        def encoder_working(accum):
            input_grad, weight_grad = block_backward(block_input, enc_kernel, stamp_one, merged)
            return (accum + weight_grad, input_grad + merged)

        def encoder_resting(accum):
            return (accum, blank_piece)

        enc_acc, down_piece = lax.cond(active, encoder_working, encoder_resting, enc_acc)
        incoming = passed_along(down_piece, "section", -1)
        return (incoming, enc_acc)

    enc_start = jnp.zeros(enc_kernel.shape, jnp.float32)
    _, enc_acc = lax.fori_loop(0, ticks_total, encoder_back_tick, (blank_piece, enc_start))
    enc_share, dec_share = (
        lax.psum_scatter(enc_acc[None], "dp", scatter_dimension=3, tiled=True),
        lax.psum_scatter(dec_acc[None], "dp", scatter_dimension=3, tiled=True),
    )
    return (enc_share, dec_share)


def solution(mesh):
    placed = (
        P("dp", None, None, None),
        P("dp", None, None, None),
        P("dp"),
        P("section", None, None, None, None),
        P("section", None, None, None, None),
    )
    return jax.shard_map(
        shards,
        mesh=mesh,
        in_specs=placed,
        out_specs=(P("section", None, None, "dp", None), P("section", None, None, "dp", None)),
        check_vma=False,
    )
```

```python
import math

import jax
import jax.numpy as jnp
from jax import lax
from jax.sharding import PartitionSpec as P

GROUPS = 32


def passed_along(value, axis, steps):
    count = lax.axis_size(axis)
    initial, last = (max(0, -steps), min(count, count - steps))
    return lax.ppermute(value, axis, [(source, source + steps) for source in range(initial, last)])


def embed(stamps_in, channels):
    half_width = channels // 2
    frequency = jnp.exp(-math.log(10000.0) * jnp.arange(half_width, dtype=jnp.float32) / half_width)
    angles = stamps_in.astype(jnp.float32)[:, None] * frequency[None, :]
    return jnp.concatenate([jnp.sin(angles), jnp.cos(angles)], axis=1)


def activate(inputs_f32, stamps_in):
    batch_rows, height, breadth, channels = inputs_f32.shape
    grouped = inputs_f32.reshape(batch_rows, height * breadth, GROUPS, channels // GROUPS)
    group_mean = jnp.mean(grouped, axis=(1, 3), keepdims=True)
    centered = grouped - group_mean
    group_var = jnp.mean(centered * centered, axis=(1, 3), keepdims=True)
    normed = (centered * lax.rsqrt(group_var + 1e-05)).reshape(inputs_f32.shape)
    modulate = 1.0 + 0.5 * embed(stamps_in, channels)[:, None, None, :]
    return jax.nn.silu(normed * modulate)


def conv_apply(activations, weight):
    batch_rows, height, breadth, channels = activations.shape
    padded = jnp.pad(activations, ((0, 0), (1, 1), (1, 1), (0, 0)))
    summed = jnp.zeros((batch_rows * height * breadth, weight.shape[3]), jnp.float32)
    for row_off in range(3):
        for col_off in range(3):
            window = padded[:, row_off : row_off + height, col_off : col_off + breadth, :].reshape(
                -1, channels
            )
            summed = summed + jnp.dot(
                window, weight[row_off, col_off], preferred_element_type=jnp.float32
            )
    return summed.reshape(batch_rows, height, breadth, weight.shape[3])


def conv_back(cotangent, weight):
    batch_rows, height, breadth, outputs = cotangent.shape
    padded = jnp.pad(cotangent.astype(jnp.bfloat16), ((0, 0), (1, 1), (1, 1), (0, 0)))
    summed = jnp.zeros((batch_rows * height * breadth, weight.shape[2]), jnp.float32)
    for row_off in range(3):
        for col_off in range(3):
            window = padded[
                :, 2 - row_off : 2 - row_off + height, 2 - col_off : 2 - col_off + breadth, :
            ].reshape(-1, outputs)
            summed = summed + lax.dot_general(
                window,
                weight[row_off, col_off],
                (((1,), (1,)), ((), ())),
                preferred_element_type=jnp.float32,
            )
    return summed.reshape(batch_rows, height, breadth, weight.shape[2])


def conv_weight_grad(activations, cotangent):
    batch_rows, height, breadth, channels = activations.shape
    padded = jnp.pad(activations, ((0, 0), (1, 1), (1, 1), (0, 0)))
    flat_cot = cotangent.astype(jnp.bfloat16).reshape(-1, cotangent.shape[3])
    kernel_rows = []
    for row_off in range(3):
        kernel_cols = []
        for col_off in range(3):
            window = padded[:, row_off : row_off + height, col_off : col_off + breadth, :].reshape(
                -1, channels
            )
            kernel_cols.append(
                lax.dot_general(
                    window, flat_cot, (((0,), (0,)), ((), ())), preferred_element_type=jnp.float32
                )
            )
        kernel_rows.append(jnp.stack(kernel_cols))
    return jnp.stack(kernel_rows)


def block_forward(inputs, residual, weight, stamps_in):
    activations = activate(inputs, stamps_in).astype(jnp.bfloat16)
    return residual + conv_apply(activations, weight)


def block_backward(inputs, weight, stamps_in, cotangent):
    activated, pullback = jax.vjp(lambda inner_field: activate(inner_field, stamps_in), inputs)
    activations = activated.astype(jnp.bfloat16)
    weight_grad = conv_weight_grad(activations, cotangent)
    input_grad = pullback(conv_back(cotangent, weight))[0]
    return (input_grad, weight_grad)


def noise_levels(stamps_in):
    phase = (stamps_in.astype(jnp.float32) / 1000.0 + 0.008) / 1.008 * (math.pi / 2.0)
    signal = jnp.cos(phase) ** 2
    return (jnp.sqrt(signal), jnp.sqrt(1.0 - signal))


def pick_row(buffer, slot_index):
    return lax.dynamic_slice_in_dim(buffer, slot_index, 1, 0)


def put_row(buffer, piece, slot_index):
    return lax.dynamic_update_slice_in_dim(buffer, piece.astype(buffer.dtype), slot_index, 0)


def shards(clean, noise, stamps, enc_weight, dec_weight):
    sections = lax.axis_size("section")
    section_index = lax.axis_index("section")
    last_section = sections - 1
    samples = clean.shape[0]
    channels = clean.shape[3]
    enc_kernel = enc_weight[0]
    dec_kernel = dec_weight[0]
    keep_level, spread_level = noise_levels(stamps)
    noisy = keep_level[:, None, None, None] * clean.astype(jnp.float32) + spread_level[
        :, None, None, None
    ] * noise.astype(jnp.float32)
    factor = 1.0 / math.sqrt(samples * lax.axis_size("dp") * clean.shape[1] * clean.shape[2])
    ticks_total = samples + sections - 1
    blank_piece = jnp.zeros((1,) + clean.shape[1:], jnp.float32)

    def locate(tick_now, offset):
        sample_id = tick_now - offset
        active = (sample_id >= 0) & (sample_id < samples)
        slot_index = jnp.clip(sample_id, -1, samples) + 1
        return (active, jnp.clip(sample_id, 0, samples - 1), slot_index)

    def padded(inner_shape, dtype=jnp.float32):
        return jnp.zeros((samples + 2,) + inner_shape, dtype)

    def real_rows(buffer):
        return buffer[1 : samples + 1]

    row_shape = clean.shape[1:]
    wide_shape = row_shape[:-1] + (2 * channels,)

    def encoder_tick(tick_now, carried):
        incoming, enc_inputs, skips = carried
        active, sample_at, slot_index = locate(tick_now, section_index)
        source = jnp.where(section_index == 0, pick_row(noisy, sample_at), incoming)
        stamp_one = pick_row(stamps, sample_at)
        result = lax.cond(
            active,
            lambda: block_forward(source, source, enc_kernel, stamp_one),
            lambda: blank_piece,
        )
        enc_inputs = put_row(enc_inputs, source, slot_index)
        skips = put_row(skips, result, slot_index)
        incoming = passed_along(result, "section", 1)
        return (incoming, enc_inputs, skips)

    _, enc_inputs, skips = lax.fori_loop(
        0, ticks_total, encoder_tick, (blank_piece, padded(row_shape), padded(row_shape))
    )

    def decoder_tick(tick_now, carried):
        incoming, dec_inputs, outputs = carried
        active, sample_at, slot_index = locate(tick_now, last_section - section_index)
        skip_piece = pick_row(skips, slot_index)
        source = jnp.where(section_index == last_section, skip_piece, incoming)
        joined = jnp.concatenate([source, skip_piece], axis=3)
        stamp_one = pick_row(stamps, sample_at)
        result = lax.cond(
            active,
            lambda: block_forward(joined, source, dec_kernel, stamp_one),
            lambda: blank_piece,
        )
        dec_inputs = put_row(dec_inputs, source, slot_index)
        outputs = put_row(outputs, result, slot_index)
        incoming = passed_along(result, "section", -1)
        return (incoming, dec_inputs, outputs)

    _, dec_inputs, outputs = lax.fori_loop(
        0, ticks_total, decoder_tick, (blank_piece, padded(row_shape), padded(row_shape))
    )

    def input_backward(inputs, weight, stamp_one, cotangent):
        activated, pullback = jax.vjp(lambda inner_field: activate(inner_field, stamp_one), inputs)
        input_grad = pullback(conv_back(cotangent, weight))[0]
        return (input_grad, activated.astype(jnp.bfloat16), cotangent.astype(jnp.bfloat16))

    def decoder_back_tick(tick_now, carried):
        incoming, skip_grads, up_grads, dec_acts, dec_cots = carried
        active, sample_at, slot_index = locate(tick_now, section_index)
        top_grad = factor * (
            pick_row(outputs, slot_index) - pick_row(noise, sample_at).astype(jnp.float32)
        )
        flowing = jnp.where(section_index == 0, top_grad, incoming)
        joined = jnp.concatenate(
            [pick_row(dec_inputs, slot_index), pick_row(skips, slot_index)], axis=3
        )
        stamp_one = pick_row(stamps, sample_at)

        def decoder_working():
            input_grad, acts, cots = input_backward(joined, dec_kernel, stamp_one, flowing)
            up_piece = input_grad[..., :channels] + flowing
            return (up_piece, input_grad[..., channels:], acts, cots)

        def decoder_resting():
            return (
                blank_piece,
                blank_piece,
                jnp.zeros((1,) + wide_shape, jnp.bfloat16),
                jnp.zeros((1,) + row_shape, jnp.bfloat16),
            )

        up_piece, skip_grad, acts, cots = lax.cond(active, decoder_working, decoder_resting)
        skip_grads = put_row(skip_grads, skip_grad, slot_index)
        up_grads = put_row(up_grads, up_piece, slot_index)
        dec_acts = put_row(dec_acts, acts, slot_index)
        dec_cots = put_row(dec_cots, cots, slot_index)
        incoming = passed_along(up_piece, "section", 1)
        return (incoming, skip_grads, up_grads, dec_acts, dec_cots)

    _, skip_grads, up_grads, dec_acts, dec_cots = lax.fori_loop(
        0,
        ticks_total,
        decoder_back_tick,
        (
            blank_piece,
            padded(row_shape),
            padded(row_shape),
            padded(wide_shape, jnp.bfloat16),
            padded(row_shape, jnp.bfloat16),
        ),
    )
    dec_acc = conv_weight_grad(real_rows(dec_acts), real_rows(dec_cots))

    def encoder_back_tick(tick_now, carried):
        incoming, enc_acts, enc_cots = carried
        active, sample_at, slot_index = locate(tick_now, last_section - section_index)
        arriving = jnp.where(
            section_index == last_section, pick_row(up_grads, slot_index), incoming
        )
        merged = arriving + pick_row(skip_grads, slot_index)
        block_input = pick_row(enc_inputs, slot_index)
        stamp_one = pick_row(stamps, sample_at)

        def encoder_working():
            input_grad, acts, cots = input_backward(block_input, enc_kernel, stamp_one, merged)
            return (input_grad + merged, acts, cots)

        def encoder_resting():
            blank_half = jnp.zeros((1,) + row_shape, jnp.bfloat16)
            return (blank_piece, blank_half, blank_half)

        down_piece, acts, cots = lax.cond(active, encoder_working, encoder_resting)
        enc_acts = put_row(enc_acts, acts, slot_index)
        enc_cots = put_row(enc_cots, cots, slot_index)
        incoming = passed_along(down_piece, "section", -1)
        return (incoming, enc_acts, enc_cots)

    _, enc_acts, enc_cots = lax.fori_loop(
        0,
        ticks_total,
        encoder_back_tick,
        (blank_piece, padded(row_shape, jnp.bfloat16), padded(row_shape, jnp.bfloat16)),
    )
    enc_acc = conv_weight_grad(real_rows(enc_acts), real_rows(enc_cots))
    enc_share, dec_share = (
        lax.psum_scatter(enc_acc[None], "dp", scatter_dimension=3, tiled=True),
        lax.psum_scatter(dec_acc[None], "dp", scatter_dimension=3, tiled=True),
    )
    return (enc_share, dec_share)


def solution(mesh):
    placed = (
        P("dp", None, None, None),
        P("dp", None, None, None),
        P("dp"),
        P("section", None, None, None, None),
        P("section", None, None, None, None),
    )
    return jax.shard_map(
        shards,
        mesh=mesh,
        in_specs=placed,
        out_specs=(P("section", None, None, "dp", None), P("section", None, None, "dp", None)),
        check_vma=False,
    )
```

```python
import math

import jax
import jax.numpy as jnp
from jax import lax
from jax.sharding import PartitionSpec as P

GROUPS = 32


def passed_along(value, axis, steps):
    count = lax.axis_size(axis)
    initial, last = (max(0, -steps), min(count, count - steps))
    return lax.ppermute(value, axis, [(source, source + steps) for source in range(initial, last)])


def embed(stamps_in, channels):
    half_width = channels // 2
    frequency = jnp.exp(-math.log(10000.0) * jnp.arange(half_width, dtype=jnp.float32) / half_width)
    angles = stamps_in.astype(jnp.float32)[:, None] * frequency[None, :]
    return jnp.concatenate([jnp.sin(angles), jnp.cos(angles)], axis=1)


def activate(inputs_f32, stamps_in):
    batch_rows, height, breadth, channels = inputs_f32.shape
    grouped = inputs_f32.reshape(batch_rows, height * breadth, GROUPS, channels // GROUPS)
    group_mean = jnp.mean(grouped, axis=(1, 3), keepdims=True)
    centered = grouped - group_mean
    group_var = jnp.mean(centered * centered, axis=(1, 3), keepdims=True)
    normed = (centered * lax.rsqrt(group_var + 1e-05)).reshape(inputs_f32.shape)
    modulate = 1.0 + 0.5 * embed(stamps_in, channels)[:, None, None, :]
    return jax.nn.silu(normed * modulate)


def conv_apply(activations, weight):
    return lax.conv_general_dilated(
        activations,
        weight,
        window_strides=(1, 1),
        padding=((1, 1), (1, 1)),
        dimension_numbers=("NHWC", "HWIO", "NHWC"),
        preferred_element_type=jnp.float32,
    )


def flipped(weight):
    return jnp.flip(weight, (0, 1)).swapaxes(2, 3)


def conv_back(cotangent, flipped_weight):
    return conv_apply(cotangent.astype(jnp.bfloat16), flipped_weight)


def conv_weight_grad(activations, cotangent):
    batch_rows, height, breadth, channels = activations.shape
    padded = jnp.pad(activations, ((0, 0), (1, 1), (1, 1), (0, 0)))
    flat_cot = cotangent.astype(jnp.bfloat16).reshape(-1, cotangent.shape[3])
    kernel_rows = []
    for row_off in range(3):
        kernel_cols = []
        for col_off in range(3):
            window = padded[:, row_off : row_off + height, col_off : col_off + breadth, :].reshape(
                -1, channels
            )
            kernel_cols.append(
                lax.dot_general(
                    window, flat_cot, (((0,), (0,)), ((), ())), preferred_element_type=jnp.float32
                )
            )
        kernel_rows.append(jnp.stack(kernel_cols))
    return jnp.stack(kernel_rows)


def block_forward(inputs, residual, weight, stamps_in):
    activations = activate(inputs, stamps_in).astype(jnp.bfloat16)
    return residual + conv_apply(activations, weight)


def noise_levels(stamps_in):
    phase = (stamps_in.astype(jnp.float32) / 1000.0 + 0.008) / 1.008 * (math.pi / 2.0)
    signal = jnp.cos(phase) ** 2
    return (jnp.sqrt(signal), jnp.sqrt(1.0 - signal))


def pick_row(buffer, slot_index):
    return lax.dynamic_slice_in_dim(buffer, slot_index, 1, 0)


def put_row(buffer, piece, slot_index):
    return lax.dynamic_update_slice_in_dim(buffer, piece.astype(buffer.dtype), slot_index, 0)


def shards(clean, noise, stamps, enc_weight, dec_weight):
    sections = lax.axis_size("section")
    section_index = lax.axis_index("section")
    last_section = sections - 1
    samples = clean.shape[0]
    channels = clean.shape[3]
    enc_kernel = enc_weight[0]
    dec_kernel = dec_weight[0]
    enc_back_kernel = flipped(enc_kernel)
    dec_back_kernel = flipped(dec_kernel)
    keep_level, spread_level = noise_levels(stamps)
    noisy = keep_level[:, None, None, None] * clean.astype(jnp.float32) + spread_level[
        :, None, None, None
    ] * noise.astype(jnp.float32)
    factor = 1.0 / math.sqrt(samples * lax.axis_size("dp") * clean.shape[1] * clean.shape[2])
    ticks_total = samples + sections - 1
    blank_piece = jnp.zeros((1,) + clean.shape[1:], jnp.float32)

    def locate(tick_now, offset):
        sample_id = tick_now - offset
        active = (sample_id >= 0) & (sample_id < samples)
        slot_index = jnp.clip(sample_id, -1, samples) + 1
        return (active, jnp.clip(sample_id, 0, samples - 1), slot_index)

    def padded(inner_shape, dtype=jnp.float32):
        return jnp.zeros((samples + 2,) + inner_shape, dtype)

    def real_rows(buffer):
        return buffer[1 : samples + 1]

    row_shape = clean.shape[1:]
    wide_shape = row_shape[:-1] + (2 * channels,)

    def encoder_tick(tick_now, carried):
        incoming, enc_inputs, skips = carried
        active, sample_at, slot_index = locate(tick_now, section_index)
        source = jnp.where(section_index == 0, pick_row(noisy, sample_at), incoming)
        stamp_one = pick_row(stamps, sample_at)
        result = lax.cond(
            active,
            lambda: block_forward(source, source, enc_kernel, stamp_one),
            lambda: blank_piece,
        )
        enc_inputs = put_row(enc_inputs, source, slot_index)
        skips = put_row(skips, result, slot_index)
        incoming = passed_along(result, "section", 1)
        return (incoming, enc_inputs, skips)

    _, enc_inputs, skips = lax.fori_loop(
        0, ticks_total, encoder_tick, (blank_piece, padded(row_shape), padded(row_shape))
    )

    def decoder_tick(tick_now, carried):
        incoming, dec_inputs, outputs = carried
        active, sample_at, slot_index = locate(tick_now, last_section - section_index)
        skip_piece = pick_row(skips, slot_index)
        source = jnp.where(section_index == last_section, skip_piece, incoming)
        joined = jnp.concatenate([source, skip_piece], axis=3)
        stamp_one = pick_row(stamps, sample_at)
        result = lax.cond(
            active,
            lambda: block_forward(joined, source, dec_kernel, stamp_one),
            lambda: blank_piece,
        )
        dec_inputs = put_row(dec_inputs, source, slot_index)
        outputs = put_row(outputs, result, slot_index)
        incoming = passed_along(result, "section", -1)
        return (incoming, dec_inputs, outputs)

    _, dec_inputs, outputs = lax.fori_loop(
        0, ticks_total, decoder_tick, (blank_piece, padded(row_shape), padded(row_shape))
    )

    def input_backward(inputs, weight, stamp_one, cotangent):
        activated, pullback = jax.vjp(lambda inner_field: activate(inner_field, stamp_one), inputs)
        input_grad = pullback(conv_back(cotangent, weight))[0]
        return (input_grad, activated.astype(jnp.bfloat16), cotangent.astype(jnp.bfloat16))

    def decoder_back_tick(tick_now, carried):
        incoming, skip_grads, up_grads, dec_acts, dec_cots = carried
        active, sample_at, slot_index = locate(tick_now, section_index)
        top_grad = factor * (
            pick_row(outputs, slot_index) - pick_row(noise, sample_at).astype(jnp.float32)
        )
        flowing = jnp.where(section_index == 0, top_grad, incoming)
        joined = jnp.concatenate(
            [pick_row(dec_inputs, slot_index), pick_row(skips, slot_index)], axis=3
        )
        stamp_one = pick_row(stamps, sample_at)

        def decoder_working():
            input_grad, acts, cots = input_backward(joined, dec_back_kernel, stamp_one, flowing)
            up_piece = input_grad[..., :channels] + flowing
            return (up_piece, input_grad[..., channels:], acts, cots)

        def decoder_resting():
            return (
                blank_piece,
                blank_piece,
                jnp.zeros((1,) + wide_shape, jnp.bfloat16),
                jnp.zeros((1,) + row_shape, jnp.bfloat16),
            )

        up_piece, skip_grad, acts, cots = lax.cond(active, decoder_working, decoder_resting)
        skip_grads = put_row(skip_grads, skip_grad, slot_index)
        up_grads = put_row(up_grads, up_piece, slot_index)
        dec_acts = put_row(dec_acts, acts, slot_index)
        dec_cots = put_row(dec_cots, cots, slot_index)
        incoming = passed_along(up_piece, "section", 1)
        return (incoming, skip_grads, up_grads, dec_acts, dec_cots)

    _, skip_grads, up_grads, dec_acts, dec_cots = lax.fori_loop(
        0,
        ticks_total,
        decoder_back_tick,
        (
            blank_piece,
            padded(row_shape),
            padded(row_shape),
            padded(wide_shape, jnp.bfloat16),
            padded(row_shape, jnp.bfloat16),
        ),
    )
    dec_acc = conv_weight_grad(real_rows(dec_acts), real_rows(dec_cots))

    def encoder_back_tick(tick_now, carried):
        incoming, enc_acts, enc_cots = carried
        active, sample_at, slot_index = locate(tick_now, last_section - section_index)
        arriving = jnp.where(
            section_index == last_section, pick_row(up_grads, slot_index), incoming
        )
        merged = arriving + pick_row(skip_grads, slot_index)
        block_input = pick_row(enc_inputs, slot_index)
        stamp_one = pick_row(stamps, sample_at)

        def encoder_working():
            input_grad, acts, cots = input_backward(block_input, enc_back_kernel, stamp_one, merged)
            return (input_grad + merged, acts, cots)

        def encoder_resting():
            blank_half = jnp.zeros((1,) + row_shape, jnp.bfloat16)
            return (blank_piece, blank_half, blank_half)

        down_piece, acts, cots = lax.cond(active, encoder_working, encoder_resting)
        enc_acts = put_row(enc_acts, acts, slot_index)
        enc_cots = put_row(enc_cots, cots, slot_index)
        incoming = passed_along(down_piece, "section", -1)
        return (incoming, enc_acts, enc_cots)

    _, enc_acts, enc_cots = lax.fori_loop(
        0,
        ticks_total,
        encoder_back_tick,
        (blank_piece, padded(row_shape, jnp.bfloat16), padded(row_shape, jnp.bfloat16)),
    )
    enc_acc = conv_weight_grad(real_rows(enc_acts), real_rows(enc_cots))
    enc_share, dec_share = (
        lax.psum_scatter(enc_acc[None], "dp", scatter_dimension=3, tiled=True),
        lax.psum_scatter(dec_acc[None], "dp", scatter_dimension=3, tiled=True),
    )
    return (enc_share, dec_share)


def solution(mesh):
    placed = (
        P("dp", None, None, None),
        P("dp", None, None, None),
        P("dp"),
        P("section", None, None, None, None),
        P("section", None, None, None, None),
    )
    return jax.shard_map(
        shards,
        mesh=mesh,
        in_specs=placed,
        out_specs=(P("section", None, None, "dp", None), P("section", None, None, "dp", None)),
        check_vma=False,
    )
```

```python
import math

import jax
import jax.numpy as jnp
from jax import lax
from jax.sharding import PartitionSpec as P

GROUPS = 32


def passed_along(value, axis, steps):
    count = lax.axis_size(axis)
    initial, last = (max(0, -steps), min(count, count - steps))
    return lax.ppermute(value, axis, [(source, source + steps) for source in range(initial, last)])


def embed(stamps_in, channels):
    half_width = channels // 2
    frequency = jnp.exp(-math.log(10000.0) * jnp.arange(half_width, dtype=jnp.float32) / half_width)
    angles = stamps_in.astype(jnp.float32)[:, None] * frequency[None, :]
    return jnp.concatenate([jnp.sin(angles), jnp.cos(angles)], axis=1)


def activate(inputs_f32, stamps_in):
    batch_rows, height, breadth, channels = inputs_f32.shape
    grouped = inputs_f32.reshape(batch_rows, height * breadth, GROUPS, channels // GROUPS)
    group_mean = jnp.mean(grouped, axis=(1, 3), keepdims=True)
    centered = grouped - group_mean
    group_var = jnp.mean(centered * centered, axis=(1, 3), keepdims=True)
    normed = (centered * lax.rsqrt(group_var + 1e-05)).reshape(inputs_f32.shape)
    modulate = 1.0 + 0.5 * embed(stamps_in, channels)[:, None, None, :]
    return jax.nn.silu(normed * modulate)


def conv_apply(activations, weight):
    return lax.conv_general_dilated(
        activations,
        weight,
        window_strides=(1, 1),
        padding=((1, 1), (1, 1)),
        dimension_numbers=("NHWC", "HWIO", "NHWC"),
        preferred_element_type=jnp.float32,
    )


def flipped(weight):
    return jnp.flip(weight, (0, 1)).swapaxes(2, 3)


def conv_back(cotangent, flipped_weight):
    return conv_apply(cotangent.astype(jnp.bfloat16), flipped_weight)


def conv_weight_grad(activations, cotangent):
    batch_rows, height, breadth, channels = activations.shape
    padded = jnp.pad(activations, ((0, 0), (1, 1), (1, 1), (0, 0)))
    flat_cot = cotangent.astype(jnp.bfloat16).reshape(-1, cotangent.shape[3])
    kernel_rows = []
    for row_off in range(3):
        kernel_cols = []
        for col_off in range(3):
            window = padded[:, row_off : row_off + height, col_off : col_off + breadth, :].reshape(
                -1, channels
            )
            kernel_cols.append(
                lax.dot_general(
                    window, flat_cot, (((0,), (0,)), ((), ())), preferred_element_type=jnp.float32
                )
            )
        kernel_rows.append(jnp.stack(kernel_cols))
    return jnp.stack(kernel_rows)


def block_forward(inputs, residual, weight, stamps_in):
    activations = activate(inputs, stamps_in).astype(jnp.bfloat16)
    return residual + conv_apply(activations, weight)


def noise_levels(stamps_in):
    phase = (stamps_in.astype(jnp.float32) / 1000.0 + 0.008) / 1.008 * (math.pi / 2.0)
    signal = jnp.cos(phase) ** 2
    return (jnp.sqrt(signal), jnp.sqrt(1.0 - signal))


def pick_row(buffer, slot_index):
    return lax.dynamic_slice_in_dim(buffer, slot_index, 1, 0)


def put_row(buffer, piece, slot_index):
    return lax.dynamic_update_slice_in_dim(buffer, piece.astype(buffer.dtype), slot_index, 0)


def shards(clean, noise, stamps, enc_weight, dec_weight):
    sections = lax.axis_size("section")
    section_index = lax.axis_index("section")
    last_section = sections - 1
    samples = clean.shape[0]
    channels = clean.shape[3]
    enc_kernel = enc_weight[0]
    dec_kernel = dec_weight[0]
    enc_back_kernel = flipped(enc_kernel)
    dec_back_kernel = flipped(dec_kernel)
    keep_level, spread_level = noise_levels(stamps)
    noisy = keep_level[:, None, None, None] * clean.astype(jnp.float32) + spread_level[
        :, None, None, None
    ] * noise.astype(jnp.float32)
    factor = 1.0 / math.sqrt(samples * lax.axis_size("dp") * clean.shape[1] * clean.shape[2])
    ticks_total = samples + sections - 1
    blank_piece = jnp.zeros((1,) + clean.shape[1:], jnp.float32)

    def locate(tick_now, offset):
        sample_id = tick_now - offset
        active = (sample_id >= 0) & (sample_id < samples)
        slot_index = jnp.clip(sample_id, -1, samples) + 1
        return (active, jnp.clip(sample_id, 0, samples - 1), slot_index)

    def padded(inner_shape, dtype=jnp.float32):
        return jnp.zeros((samples + 2,) + inner_shape, dtype)

    def real_rows(buffer):
        return buffer[1 : samples + 1]

    row_shape = clean.shape[1:]
    wide_shape = row_shape[:-1] + (2 * channels,)

    def encoder_tick(tick_now, carried):
        incoming, enc_inputs, skips = carried
        active, sample_at, slot_index = locate(tick_now, section_index)
        source = jnp.where(section_index == 0, pick_row(noisy, sample_at), incoming)
        stamp_one = pick_row(stamps, sample_at)
        result = lax.cond(
            active,
            lambda: block_forward(source, source, enc_kernel, stamp_one),
            lambda: blank_piece,
        )
        enc_inputs = put_row(enc_inputs, source, slot_index)
        skips = put_row(skips, result, slot_index)
        incoming = passed_along(result, "section", 1)
        return (incoming, enc_inputs, skips)

    _, enc_inputs, skips = lax.fori_loop(
        0, ticks_total, encoder_tick, (blank_piece, padded(row_shape), padded(row_shape))
    )

    def decoder_tick(tick_now, carried):
        incoming, dec_inputs, outputs = carried
        active, sample_at, slot_index = locate(tick_now, last_section - section_index)
        skip_piece = pick_row(skips, slot_index)
        source = jnp.where(section_index == last_section, skip_piece, incoming)
        joined = jnp.concatenate([source, skip_piece], axis=3)
        stamp_one = pick_row(stamps, sample_at)
        result = lax.cond(
            active,
            lambda: block_forward(joined, source, dec_kernel, stamp_one),
            lambda: blank_piece,
        )
        dec_inputs = put_row(dec_inputs, source, slot_index)
        outputs = put_row(outputs, result, slot_index)
        incoming = passed_along(result, "section", -1)
        return (incoming, dec_inputs, outputs)

    _, dec_inputs, outputs = lax.fori_loop(
        0, ticks_total, decoder_tick, (blank_piece, padded(row_shape), padded(row_shape))
    )

    def input_backward(inputs, weight, stamp_one, cotangent):
        activated, pullback = jax.vjp(lambda inner_field: activate(inner_field, stamp_one), inputs)
        input_grad = pullback(conv_back(cotangent, weight))[0]
        return (input_grad, activated.astype(jnp.bfloat16), cotangent.astype(jnp.bfloat16))

    def decoder_back_tick(tick_now, carried):
        incoming, skip_grads, up_grads, dec_acts, dec_cots = carried
        active, sample_at, slot_index = locate(tick_now, section_index)
        top_grad = factor * (
            pick_row(outputs, slot_index) - pick_row(noise, sample_at).astype(jnp.float32)
        )
        flowing = jnp.where(section_index == 0, top_grad, incoming)
        joined = jnp.concatenate(
            [pick_row(dec_inputs, slot_index), pick_row(skips, slot_index)], axis=3
        )
        stamp_one = pick_row(stamps, sample_at)

        def decoder_working():
            input_grad, acts, cots = input_backward(joined, dec_back_kernel, stamp_one, flowing)
            up_piece = input_grad[..., :channels] + flowing
            return (up_piece, input_grad[..., channels:], acts, cots)

        def decoder_resting():
            return (
                blank_piece,
                blank_piece,
                jnp.zeros((1,) + wide_shape, jnp.bfloat16),
                jnp.zeros((1,) + row_shape, jnp.bfloat16),
            )

        up_piece, skip_grad, acts, cots = lax.cond(active, decoder_working, decoder_resting)
        skip_grads = put_row(skip_grads, skip_grad, slot_index)
        up_grads = put_row(up_grads, up_piece, slot_index)
        dec_acts = put_row(dec_acts, acts, slot_index)
        dec_cots = put_row(dec_cots, cots, slot_index)
        incoming = passed_along(up_piece, "section", 1)
        return (incoming, skip_grads, up_grads, dec_acts, dec_cots)

    _, skip_grads, up_grads, dec_acts, dec_cots = lax.fori_loop(
        0,
        ticks_total,
        decoder_back_tick,
        (
            blank_piece,
            padded(row_shape),
            padded(row_shape),
            padded(wide_shape, jnp.bfloat16),
            padded(row_shape, jnp.bfloat16),
        ),
    )
    dec_acc = conv_weight_grad(real_rows(dec_acts), real_rows(dec_cots))

    def encoder_back_tick(tick_now, carried):
        incoming, enc_acts, enc_cots = carried
        active, sample_at, slot_index = locate(tick_now, last_section - section_index)
        arriving = jnp.where(
            section_index == last_section, pick_row(up_grads, slot_index), incoming
        )
        merged = arriving + pick_row(skip_grads, slot_index)
        block_input = pick_row(enc_inputs, slot_index)
        stamp_one = pick_row(stamps, sample_at)

        def encoder_working():
            input_grad, acts, cots = input_backward(block_input, enc_back_kernel, stamp_one, merged)
            return (input_grad + merged, acts, cots)

        def encoder_resting():
            blank_half = jnp.zeros((1,) + row_shape, jnp.bfloat16)
            return (blank_piece, blank_half, blank_half)

        down_piece, acts, cots = lax.cond(active, encoder_working, encoder_resting)
        enc_acts = put_row(enc_acts, acts, slot_index)
        enc_cots = put_row(enc_cots, cots, slot_index)
        incoming = passed_along(down_piece, "section", -1)
        return (incoming, enc_acts, enc_cots)

    _, enc_acts, enc_cots = lax.fori_loop(
        0,
        ticks_total,
        encoder_back_tick,
        (blank_piece, padded(row_shape, jnp.bfloat16), padded(row_shape, jnp.bfloat16)),
    )
    enc_acc = conv_weight_grad(real_rows(enc_acts), real_rows(enc_cots))
    replicas = lax.axis_size("dp")
    enc_rows = enc_acc.shape[2] // replicas
    dec_rows = dec_acc.shape[2] // replicas
    both = jnp.concatenate(
        [
            enc_acc.reshape(3, 3, replicas, enc_rows, -1),
            dec_acc.reshape(3, 3, replicas, dec_rows, -1),
        ],
        axis=3,
    ).reshape(1, 3, 3, replicas * (enc_rows + dec_rows), -1)
    share = lax.psum_scatter(both, "dp", scatter_dimension=3, tiled=True)
    enc_share = share[:, :, :, :enc_rows]
    dec_share = share[:, :, :, enc_rows:]
    return (enc_share, dec_share)


def solution(mesh):
    placed = (
        P("dp", None, None, None),
        P("dp", None, None, None),
        P("dp"),
        P("section", None, None, None, None),
        P("section", None, None, None, None),
    )
    return jax.shard_map(
        shards,
        mesh=mesh,
        in_specs=placed,
        out_specs=(P("section", None, None, "dp", None), P("section", None, None, "dp", None)),
        check_vma=False,
    )
```

```python
import math

import jax
import jax.numpy as jnp
from jax import lax
from jax.sharding import PartitionSpec as P

GROUPS = 32


def passed_along(value, axis, steps):
    count = lax.axis_size(axis)
    initial, last = (max(0, -steps), min(count, count - steps))
    return lax.ppermute(value, axis, [(source, source + steps) for source in range(initial, last)])


def embed(stamps_in, channels):
    half_width = channels // 2
    frequency = jnp.exp(-math.log(10000.0) * jnp.arange(half_width, dtype=jnp.float32) / half_width)
    angles = stamps_in.astype(jnp.float32)[:, None] * frequency[None, :]
    return jnp.concatenate([jnp.sin(angles), jnp.cos(angles)], axis=1)


def activate(inputs_f32, modulate_row):
    batch_rows, height, breadth, channels = inputs_f32.shape
    grouped = inputs_f32.reshape(batch_rows, height * breadth, GROUPS, channels // GROUPS)
    group_mean = jnp.mean(grouped, axis=(1, 3), keepdims=True)
    centered = grouped - group_mean
    group_var = jnp.mean(centered * centered, axis=(1, 3), keepdims=True)
    normed = (centered * lax.rsqrt(group_var + 1e-05)).reshape(inputs_f32.shape)
    return jax.nn.silu(normed * modulate_row[:, None, None, :])


def conv_apply(activations, weight):
    return lax.conv_general_dilated(
        activations,
        weight,
        window_strides=(1, 1),
        padding=((1, 1), (1, 1)),
        dimension_numbers=("NHWC", "HWIO", "NHWC"),
        preferred_element_type=jnp.float32,
    )


def flipped(weight):
    return jnp.flip(weight, (0, 1)).swapaxes(2, 3)


def conv_back(cotangent, flipped_weight):
    return conv_apply(cotangent.astype(jnp.bfloat16), flipped_weight)


def conv_weight_grad(activations, cotangent):
    batch_rows, height, breadth, channels = activations.shape
    padded = jnp.pad(activations, ((0, 0), (1, 1), (1, 1), (0, 0)))
    flat_cot = cotangent.astype(jnp.bfloat16).reshape(-1, cotangent.shape[3])
    kernel_rows = []
    for row_off in range(3):
        kernel_cols = []
        for col_off in range(3):
            window = padded[:, row_off : row_off + height, col_off : col_off + breadth, :].reshape(
                -1, channels
            )
            kernel_cols.append(
                lax.dot_general(
                    window, flat_cot, (((0,), (0,)), ((), ())), preferred_element_type=jnp.float32
                )
            )
        kernel_rows.append(jnp.stack(kernel_cols))
    return jnp.stack(kernel_rows)


def modulation(stamps_in, channels):
    return 1.0 + 0.5 * embed(stamps_in, channels)


def chosen_row(table, sample_at):
    hit = (jnp.arange(table.shape[0]) == sample_at)[:, None]
    return jnp.sum(jnp.where(hit, table, 0.0), axis=0, keepdims=True)


def block_forward(inputs, residual, weight, modulate_row):
    activations = activate(inputs, modulate_row).astype(jnp.bfloat16)
    return residual + conv_apply(activations, weight)


def noise_levels(stamps_in):
    phase = (stamps_in.astype(jnp.float32) / 1000.0 + 0.008) / 1.008 * (math.pi / 2.0)
    signal = jnp.cos(phase) ** 2
    return (jnp.sqrt(signal), jnp.sqrt(1.0 - signal))


def pick_row(buffer, slot_index):
    return lax.dynamic_slice_in_dim(buffer, slot_index, 1, 0)


def put_row(buffer, piece, slot_index):
    return lax.dynamic_update_slice_in_dim(buffer, piece.astype(buffer.dtype), slot_index, 0)


def shards(clean, noise, stamps, enc_weight, dec_weight):
    sections = lax.axis_size("section")
    section_index = lax.axis_index("section")
    last_section = sections - 1
    samples = clean.shape[0]
    channels = clean.shape[3]
    enc_kernel = enc_weight[0]
    dec_kernel = dec_weight[0]
    narrow_table = modulation(stamps, channels)
    wide_table = modulation(stamps, 2 * channels)
    enc_back_kernel = flipped(enc_kernel)
    dec_back_kernel = flipped(dec_kernel)
    keep_level, spread_level = noise_levels(stamps)
    noisy = keep_level[:, None, None, None] * clean.astype(jnp.float32) + spread_level[
        :, None, None, None
    ] * noise.astype(jnp.float32)
    factor = 1.0 / math.sqrt(samples * lax.axis_size("dp") * clean.shape[1] * clean.shape[2])
    ticks_total = samples + sections - 1
    blank_piece = jnp.zeros((1,) + clean.shape[1:], jnp.float32)

    def locate(tick_now, offset):
        sample_id = tick_now - offset
        active = (sample_id >= 0) & (sample_id < samples)
        slot_index = jnp.clip(sample_id, -1, samples) + 1
        return (active, jnp.clip(sample_id, 0, samples - 1), slot_index)

    def padded(inner_shape, dtype=jnp.float32):
        return jnp.zeros((samples + 2,) + inner_shape, dtype)

    def real_rows(buffer):
        return buffer[1 : samples + 1]

    row_shape = clean.shape[1:]
    wide_shape = row_shape[:-1] + (2 * channels,)

    def encoder_tick(tick_now, carried):
        incoming, enc_inputs, skips = carried
        active, sample_at, slot_index = locate(tick_now, section_index)
        source = jnp.where(section_index == 0, pick_row(noisy, sample_at), incoming)
        stamp_one = chosen_row(narrow_table, sample_at)
        result = lax.cond(
            active,
            lambda: block_forward(source, source, enc_kernel, stamp_one),
            lambda: blank_piece,
        )
        enc_inputs = put_row(enc_inputs, source, slot_index)
        skips = put_row(skips, result, slot_index)
        incoming = passed_along(result, "section", 1)
        return (incoming, enc_inputs, skips)

    _, enc_inputs, skips = lax.fori_loop(
        0, ticks_total, encoder_tick, (blank_piece, padded(row_shape), padded(row_shape))
    )

    def decoder_tick(tick_now, carried):
        incoming, dec_inputs, outputs = carried
        active, sample_at, slot_index = locate(tick_now, last_section - section_index)
        skip_piece = pick_row(skips, slot_index)
        source = jnp.where(section_index == last_section, skip_piece, incoming)
        joined = jnp.concatenate([source, skip_piece], axis=3)
        stamp_one = chosen_row(wide_table, sample_at)
        result = lax.cond(
            active,
            lambda: block_forward(joined, source, dec_kernel, stamp_one),
            lambda: blank_piece,
        )
        dec_inputs = put_row(dec_inputs, source, slot_index)
        outputs = put_row(outputs, result, slot_index)
        incoming = passed_along(result, "section", -1)
        return (incoming, dec_inputs, outputs)

    _, dec_inputs, outputs = lax.fori_loop(
        0, ticks_total, decoder_tick, (blank_piece, padded(row_shape), padded(row_shape))
    )

    def input_backward(inputs, weight, stamp_one, cotangent):
        activated, pullback = jax.vjp(lambda inner_field: activate(inner_field, stamp_one), inputs)
        input_grad = pullback(conv_back(cotangent, weight))[0]
        return (input_grad, activated.astype(jnp.bfloat16), cotangent.astype(jnp.bfloat16))

    def decoder_back_tick(tick_now, carried):
        incoming, skip_grads, up_grads, dec_acts, dec_cots = carried
        active, sample_at, slot_index = locate(tick_now, section_index)
        top_grad = factor * (
            pick_row(outputs, slot_index) - pick_row(noise, sample_at).astype(jnp.float32)
        )
        flowing = jnp.where(section_index == 0, top_grad, incoming)
        joined = jnp.concatenate(
            [pick_row(dec_inputs, slot_index), pick_row(skips, slot_index)], axis=3
        )
        stamp_one = chosen_row(wide_table, sample_at)

        def decoder_working():
            input_grad, acts, cots = input_backward(joined, dec_back_kernel, stamp_one, flowing)
            up_piece = input_grad[..., :channels] + flowing
            return (up_piece, input_grad[..., channels:], acts, cots)

        def decoder_resting():
            return (
                blank_piece,
                blank_piece,
                jnp.zeros((1,) + wide_shape, jnp.bfloat16),
                jnp.zeros((1,) + row_shape, jnp.bfloat16),
            )

        up_piece, skip_grad, acts, cots = lax.cond(active, decoder_working, decoder_resting)
        skip_grads = put_row(skip_grads, skip_grad, slot_index)
        up_grads = put_row(up_grads, up_piece, slot_index)
        dec_acts = put_row(dec_acts, acts, slot_index)
        dec_cots = put_row(dec_cots, cots, slot_index)
        incoming = passed_along(up_piece, "section", 1)
        return (incoming, skip_grads, up_grads, dec_acts, dec_cots)

    _, skip_grads, up_grads, dec_acts, dec_cots = lax.fori_loop(
        0,
        ticks_total,
        decoder_back_tick,
        (
            blank_piece,
            padded(row_shape),
            padded(row_shape),
            padded(wide_shape, jnp.bfloat16),
            padded(row_shape, jnp.bfloat16),
        ),
    )
    dec_acc = conv_weight_grad(real_rows(dec_acts), real_rows(dec_cots))

    def encoder_back_tick(tick_now, carried):
        incoming, enc_acts, enc_cots = carried
        active, sample_at, slot_index = locate(tick_now, last_section - section_index)
        arriving = jnp.where(
            section_index == last_section, pick_row(up_grads, slot_index), incoming
        )
        merged = arriving + pick_row(skip_grads, slot_index)
        block_input = pick_row(enc_inputs, slot_index)
        stamp_one = chosen_row(narrow_table, sample_at)

        def encoder_working():
            input_grad, acts, cots = input_backward(block_input, enc_back_kernel, stamp_one, merged)
            return (input_grad + merged, acts, cots)

        def encoder_resting():
            blank_half = jnp.zeros((1,) + row_shape, jnp.bfloat16)
            return (blank_piece, blank_half, blank_half)

        down_piece, acts, cots = lax.cond(active, encoder_working, encoder_resting)
        enc_acts = put_row(enc_acts, acts, slot_index)
        enc_cots = put_row(enc_cots, cots, slot_index)
        incoming = passed_along(down_piece, "section", -1)
        return (incoming, enc_acts, enc_cots)

    _, enc_acts, enc_cots = lax.fori_loop(
        0,
        ticks_total,
        encoder_back_tick,
        (blank_piece, padded(row_shape, jnp.bfloat16), padded(row_shape, jnp.bfloat16)),
    )
    enc_acc = conv_weight_grad(real_rows(enc_acts), real_rows(enc_cots))
    replicas = lax.axis_size("dp")
    enc_rows = enc_acc.shape[2] // replicas
    dec_rows = dec_acc.shape[2] // replicas
    both = jnp.concatenate(
        [
            enc_acc.reshape(3, 3, replicas, enc_rows, -1),
            dec_acc.reshape(3, 3, replicas, dec_rows, -1),
        ],
        axis=3,
    ).reshape(1, 3, 3, replicas * (enc_rows + dec_rows), -1)
    share = lax.psum_scatter(both, "dp", scatter_dimension=3, tiled=True)
    enc_share = share[:, :, :, :enc_rows]
    dec_share = share[:, :, :, enc_rows:]
    return (enc_share, dec_share)


def solution(mesh):
    placed = (
        P("dp", None, None, None),
        P("dp", None, None, None),
        P("dp"),
        P("section", None, None, None, None),
        P("section", None, None, None, None),
    )
    return jax.shard_map(
        shards,
        mesh=mesh,
        in_specs=placed,
        out_specs=(P("section", None, None, "dp", None), P("section", None, None, "dp", None)),
        check_vma=False,
    )
```

```python
import math

import jax
import jax.numpy as jnp
from jax import lax
from jax.sharding import PartitionSpec as P

GROUPS = 32


def passed_along(value, axis, steps):
    count = lax.axis_size(axis)
    initial, last = (max(0, -steps), min(count, count - steps))
    return lax.ppermute(value, axis, [(source, source + steps) for source in range(initial, last)])


def crossing_pairs(steps):
    sections = lax.axis_size("section")
    replicas = lax.axis_size("dp")
    half, flip = (sections // 2, replicas // 2)
    pairs = []
    for source in range(max(0, -steps), min(sections, sections - steps)):
        target = source + steps
        crosses = (source < half) != (target < half)
        for replica in range(replicas):
            other = (replica + flip) % replicas if crosses else replica
            pairs.append((source * replicas + replica, target * replicas + other))
    return pairs


def passed_across(value, steps):
    return lax.ppermute(value, ("section", "dp"), crossing_pairs(steps))


def embed(stamps_in, channels):
    half_width = channels // 2
    frequency = jnp.exp(-math.log(10000.0) * jnp.arange(half_width, dtype=jnp.float32) / half_width)
    angles = stamps_in.astype(jnp.float32)[:, None] * frequency[None, :]
    return jnp.concatenate([jnp.sin(angles), jnp.cos(angles)], axis=1)


def activate(inputs_f32, modulate_row):
    batch_rows, height, breadth, channels = inputs_f32.shape
    grouped = inputs_f32.reshape(batch_rows, height * breadth, GROUPS, channels // GROUPS)
    group_mean = jnp.mean(grouped, axis=(1, 3), keepdims=True)
    centered = grouped - group_mean
    group_var = jnp.mean(centered * centered, axis=(1, 3), keepdims=True)
    normed = (centered * lax.rsqrt(group_var + 1e-05)).reshape(inputs_f32.shape)
    return jax.nn.silu(normed * modulate_row[:, None, None, :])


def conv_apply(activations, weight):
    return lax.conv_general_dilated(
        activations,
        weight,
        window_strides=(1, 1),
        padding=((1, 1), (1, 1)),
        dimension_numbers=("NHWC", "HWIO", "NHWC"),
        preferred_element_type=jnp.float32,
    )


def flipped(weight):
    return jnp.flip(weight, (0, 1)).swapaxes(2, 3)


def conv_back(cotangent, flipped_weight):
    return conv_apply(cotangent.astype(jnp.bfloat16), flipped_weight)


def conv_weight_grad(activations, cotangent):
    batch_rows, height, breadth, channels = activations.shape
    padded = jnp.pad(activations, ((0, 0), (1, 1), (1, 1), (0, 0)))
    flat_cot = cotangent.astype(jnp.bfloat16).reshape(-1, cotangent.shape[3])
    kernel_rows = []
    for row_off in range(3):
        kernel_cols = []
        for col_off in range(3):
            window = padded[:, row_off : row_off + height, col_off : col_off + breadth, :].reshape(
                -1, channels
            )
            kernel_cols.append(
                lax.dot_general(
                    window, flat_cot, (((0,), (0,)), ((), ())), preferred_element_type=jnp.float32
                )
            )
        kernel_rows.append(jnp.stack(kernel_cols))
    return jnp.stack(kernel_rows)


def modulation(stamps_in, channels):
    return 1.0 + 0.5 * embed(stamps_in, channels)


def chosen_row(table, sample_at):
    hit = (jnp.arange(table.shape[0]) == sample_at)[:, None]
    return jnp.sum(jnp.where(hit, table, 0.0), axis=0, keepdims=True)


def block_forward(inputs, residual, weight, modulate_row):
    activations = activate(inputs, modulate_row).astype(jnp.bfloat16)
    return residual + conv_apply(activations, weight)


def noise_levels(stamps_in):
    phase = (stamps_in.astype(jnp.float32) / 1000.0 + 0.008) / 1.008 * (math.pi / 2.0)
    signal = jnp.cos(phase) ** 2
    return (jnp.sqrt(signal), jnp.sqrt(1.0 - signal))


def pick_row(buffer, slot_index):
    return lax.dynamic_slice_in_dim(buffer, slot_index, 1, 0)


def put_row(buffer, piece, slot_index):
    return lax.dynamic_update_slice_in_dim(buffer, piece.astype(buffer.dtype), slot_index, 0)


def shards(clean, noise, stamps, enc_weight, dec_weight):
    sections = lax.axis_size("section")
    section_index = lax.axis_index("section")
    last_section = sections - 1
    samples = clean.shape[0]
    channels = clean.shape[3]
    enc_kernel = enc_weight[0]
    dec_kernel = dec_weight[0]
    replicas = lax.axis_size("dp")
    flipped_stamps = lax.ppermute(
        stamps.astype(jnp.float32),
        "dp",
        [(replica, (replica + replicas // 2) % replicas) for replica in range(replicas)],
    )
    held_stamps = jnp.where(section_index < sections // 2, stamps.astype(jnp.float32), flipped_stamps)
    narrow_table = modulation(held_stamps, channels)
    wide_table = modulation(held_stamps, 2 * channels)
    enc_back_kernel = flipped(enc_kernel)
    dec_back_kernel = flipped(dec_kernel)
    keep_level, spread_level = noise_levels(stamps)
    noisy = keep_level[:, None, None, None] * clean.astype(jnp.float32) + spread_level[
        :, None, None, None
    ] * noise.astype(jnp.float32)
    factor = 1.0 / math.sqrt(samples * lax.axis_size("dp") * clean.shape[1] * clean.shape[2])
    ticks_total = samples + sections - 1
    blank_piece = jnp.zeros((1,) + clean.shape[1:], jnp.float32)

    def locate(tick_now, offset):
        sample_id = tick_now - offset
        active = (sample_id >= 0) & (sample_id < samples)
        slot_index = jnp.clip(sample_id, -1, samples) + 1
        return (active, jnp.clip(sample_id, 0, samples - 1), slot_index)

    def padded(inner_shape, dtype=jnp.float32):
        return jnp.zeros((samples + 2,) + inner_shape, dtype)

    def real_rows(buffer):
        return buffer[1 : samples + 1]

    row_shape = clean.shape[1:]
    wide_shape = row_shape[:-1] + (2 * channels,)

    def encoder_tick(tick_now, carried):
        incoming, enc_inputs, skips = carried
        active, sample_at, slot_index = locate(tick_now, section_index)
        source = jnp.where(section_index == 0, pick_row(noisy, sample_at), incoming)
        stamp_one = chosen_row(narrow_table, sample_at)
        result = lax.cond(
            active,
            lambda: block_forward(source, source, enc_kernel, stamp_one),
            lambda: blank_piece,
        )
        enc_inputs = put_row(enc_inputs, source, slot_index)
        skips = put_row(skips, result, slot_index)
        incoming = passed_across(result, 1)
        return (incoming, enc_inputs, skips)

    _, enc_inputs, skips = lax.fori_loop(
        0, ticks_total, encoder_tick, (blank_piece, padded(row_shape), padded(row_shape))
    )

    def decoder_tick(tick_now, carried):
        incoming, dec_inputs, outputs = carried
        active, sample_at, slot_index = locate(tick_now, last_section - section_index)
        skip_piece = pick_row(skips, slot_index)
        source = jnp.where(section_index == last_section, skip_piece, incoming)
        joined = jnp.concatenate([source, skip_piece], axis=3)
        stamp_one = chosen_row(wide_table, sample_at)
        result = lax.cond(
            active,
            lambda: block_forward(joined, source, dec_kernel, stamp_one),
            lambda: blank_piece,
        )
        dec_inputs = put_row(dec_inputs, source, slot_index)
        outputs = put_row(outputs, result, slot_index)
        incoming = passed_across(result, -1)
        return (incoming, dec_inputs, outputs)

    _, dec_inputs, outputs = lax.fori_loop(
        0, ticks_total, decoder_tick, (blank_piece, padded(row_shape), padded(row_shape))
    )

    def input_backward(inputs, weight, stamp_one, cotangent):
        activated, pullback = jax.vjp(lambda inner_field: activate(inner_field, stamp_one), inputs)
        input_grad = pullback(conv_back(cotangent, weight))[0]
        return (input_grad, activated.astype(jnp.bfloat16), cotangent.astype(jnp.bfloat16))

    def decoder_back_tick(tick_now, carried):
        incoming, skip_grads, up_grads, dec_acts, dec_cots = carried
        active, sample_at, slot_index = locate(tick_now, section_index)
        top_grad = factor * (
            pick_row(outputs, slot_index) - pick_row(noise, sample_at).astype(jnp.float32)
        )
        flowing = jnp.where(section_index == 0, top_grad, incoming)
        joined = jnp.concatenate(
            [pick_row(dec_inputs, slot_index), pick_row(skips, slot_index)], axis=3
        )
        stamp_one = chosen_row(wide_table, sample_at)

        def decoder_working():
            input_grad, acts, cots = input_backward(joined, dec_back_kernel, stamp_one, flowing)
            up_piece = input_grad[..., :channels] + flowing
            return (up_piece, input_grad[..., channels:], acts, cots)

        def decoder_resting():
            return (
                blank_piece,
                blank_piece,
                jnp.zeros((1,) + wide_shape, jnp.bfloat16),
                jnp.zeros((1,) + row_shape, jnp.bfloat16),
            )

        up_piece, skip_grad, acts, cots = lax.cond(active, decoder_working, decoder_resting)
        skip_grads = put_row(skip_grads, skip_grad, slot_index)
        up_grads = put_row(up_grads, up_piece, slot_index)
        dec_acts = put_row(dec_acts, acts, slot_index)
        dec_cots = put_row(dec_cots, cots, slot_index)
        incoming = passed_across(up_piece, 1)
        return (incoming, skip_grads, up_grads, dec_acts, dec_cots)

    _, skip_grads, up_grads, dec_acts, dec_cots = lax.fori_loop(
        0,
        ticks_total,
        decoder_back_tick,
        (
            blank_piece,
            padded(row_shape),
            padded(row_shape),
            padded(wide_shape, jnp.bfloat16),
            padded(row_shape, jnp.bfloat16),
        ),
    )
    dec_acc = conv_weight_grad(real_rows(dec_acts), real_rows(dec_cots))

    def encoder_back_tick(tick_now, carried):
        incoming, enc_acts, enc_cots = carried
        active, sample_at, slot_index = locate(tick_now, last_section - section_index)
        arriving = jnp.where(
            section_index == last_section, pick_row(up_grads, slot_index), incoming
        )
        merged = arriving + pick_row(skip_grads, slot_index)
        block_input = pick_row(enc_inputs, slot_index)
        stamp_one = chosen_row(narrow_table, sample_at)

        def encoder_working():
            input_grad, acts, cots = input_backward(block_input, enc_back_kernel, stamp_one, merged)
            return (input_grad + merged, acts, cots)

        def encoder_resting():
            blank_half = jnp.zeros((1,) + row_shape, jnp.bfloat16)
            return (blank_piece, blank_half, blank_half)

        down_piece, acts, cots = lax.cond(active, encoder_working, encoder_resting)
        enc_acts = put_row(enc_acts, acts, slot_index)
        enc_cots = put_row(enc_cots, cots, slot_index)
        incoming = passed_across(down_piece, -1)
        return (incoming, enc_acts, enc_cots)

    _, enc_acts, enc_cots = lax.fori_loop(
        0,
        ticks_total,
        encoder_back_tick,
        (blank_piece, padded(row_shape, jnp.bfloat16), padded(row_shape, jnp.bfloat16)),
    )
    enc_acc = conv_weight_grad(real_rows(enc_acts), real_rows(enc_cots))
    replicas = lax.axis_size("dp")
    enc_rows = enc_acc.shape[2] // replicas
    dec_rows = dec_acc.shape[2] // replicas
    both = jnp.concatenate(
        [
            enc_acc.reshape(3, 3, replicas, enc_rows, -1),
            dec_acc.reshape(3, 3, replicas, dec_rows, -1),
        ],
        axis=3,
    ).reshape(1, 3, 3, replicas * (enc_rows + dec_rows), -1)
    share = lax.psum_scatter(both, "dp", scatter_dimension=3, tiled=True)
    enc_share = share[:, :, :, :enc_rows]
    dec_share = share[:, :, :, enc_rows:]
    return (enc_share, dec_share)


def solution(mesh):
    placed = (
        P("dp", None, None, None),
        P("dp", None, None, None),
        P("dp"),
        P("section", None, None, None, None),
        P("section", None, None, None, None),
    )
    return jax.shard_map(
        shards,
        mesh=mesh,
        in_specs=placed,
        out_specs=(P("section", None, None, "dp", None), P("section", None, None, "dp", None)),
        check_vma=False,
    )
```

```python
import math

import jax
import jax.numpy as jnp
from jax import lax
from jax.sharding import PartitionSpec as P

GROUPS = 32


def passed_along(value, axis, steps):
    count = lax.axis_size(axis)
    initial, last = (max(0, -steps), min(count, count - steps))
    return lax.ppermute(value, axis, [(source, source + steps) for source in range(initial, last)])


def embed(stamps_in, channels):
    half_width = channels // 2
    frequency = jnp.exp(-math.log(10000.0) * jnp.arange(half_width, dtype=jnp.float32) / half_width)
    angles = stamps_in.astype(jnp.float32)[:, None] * frequency[None, :]
    return jnp.concatenate([jnp.sin(angles), jnp.cos(angles)], axis=1)


def activate(inputs_f32, modulate_row):
    batch_rows, height, breadth, channels = inputs_f32.shape
    grouped = inputs_f32.reshape(batch_rows, height * breadth, GROUPS, channels // GROUPS)
    group_mean = jnp.mean(grouped, axis=(1, 3), keepdims=True)
    centered = grouped - group_mean
    group_var = jnp.mean(centered * centered, axis=(1, 3), keepdims=True)
    normed = (centered * lax.rsqrt(group_var + 1e-05)).reshape(inputs_f32.shape)
    return jax.nn.silu(normed * modulate_row[:, None, None, :])


def conv_apply(activations, weight):
    return lax.conv_general_dilated(
        activations,
        weight,
        window_strides=(1, 1),
        padding=((1, 1), (1, 1)),
        dimension_numbers=("NHWC", "HWIO", "NHWC"),
        preferred_element_type=jnp.float32,
    )


def flipped(weight):
    return jnp.flip(weight, (0, 1)).swapaxes(2, 3)


def conv_back(cotangent, flipped_weight):
    return conv_apply(cotangent.astype(jnp.bfloat16), flipped_weight)


def conv_weight_grad(activations, cotangent):
    return lax.conv_general_dilated(
        activations,
        cotangent.astype(jnp.bfloat16),
        window_strides=(1, 1),
        padding=((1, 1), (1, 1)),
        dimension_numbers=("CHWN", "IHWO", "HWNC"),
        preferred_element_type=jnp.float32,
    )


def modulation(stamps_in, channels):
    return 1.0 + 0.5 * embed(stamps_in, channels)


def chosen_row(table, sample_at):
    hit = (jnp.arange(table.shape[0]) == sample_at)[:, None]
    return jnp.sum(jnp.where(hit, table, 0.0), axis=0, keepdims=True)


def block_forward(inputs, residual, weight, modulate_row):
    activations = activate(inputs, modulate_row).astype(jnp.bfloat16)
    return residual + conv_apply(activations, weight)


def noise_levels(stamps_in):
    phase = (stamps_in.astype(jnp.float32) / 1000.0 + 0.008) / 1.008 * (math.pi / 2.0)
    signal = jnp.cos(phase) ** 2
    return (jnp.sqrt(signal), jnp.sqrt(1.0 - signal))


def pick_row(buffer, slot_index):
    return lax.dynamic_slice_in_dim(buffer, slot_index, 1, 0)


def put_row(buffer, piece, slot_index):
    return lax.dynamic_update_slice_in_dim(buffer, piece.astype(buffer.dtype), slot_index, 0)


def shards(clean, noise, stamps, enc_weight, dec_weight):
    sections = lax.axis_size("section")
    section_index = lax.axis_index("section")
    last_section = sections - 1
    samples = clean.shape[0]
    channels = clean.shape[3]
    enc_kernel = enc_weight[0]
    dec_kernel = dec_weight[0]
    narrow_table = modulation(stamps, channels)
    wide_table = modulation(stamps, 2 * channels)
    enc_back_kernel = flipped(enc_kernel)
    dec_back_kernel = flipped(dec_kernel)
    keep_level, spread_level = noise_levels(stamps)
    noisy = keep_level[:, None, None, None] * clean.astype(jnp.float32) + spread_level[
        :, None, None, None
    ] * noise.astype(jnp.float32)
    factor = 1.0 / math.sqrt(samples * lax.axis_size("dp") * clean.shape[1] * clean.shape[2])
    ticks_total = samples + sections - 1
    blank_piece = jnp.zeros((1,) + clean.shape[1:], jnp.float32)

    def locate(tick_now, offset):
        sample_id = tick_now - offset
        active = (sample_id >= 0) & (sample_id < samples)
        slot_index = jnp.clip(sample_id, -1, samples) + 1
        return (active, jnp.clip(sample_id, 0, samples - 1), slot_index)

    def padded(inner_shape, dtype=jnp.float32):
        return jnp.zeros((samples + 2,) + inner_shape, dtype)

    def real_rows(buffer):
        return buffer[1 : samples + 1]

    row_shape = clean.shape[1:]
    wide_shape = row_shape[:-1] + (2 * channels,)

    def encoder_tick(tick_now, carried):
        incoming, enc_inputs, skips = carried
        active, sample_at, slot_index = locate(tick_now, section_index)
        source = jnp.where(section_index == 0, pick_row(noisy, sample_at), incoming)
        stamp_one = chosen_row(narrow_table, sample_at)
        result = lax.cond(
            active,
            lambda: block_forward(source, source, enc_kernel, stamp_one),
            lambda: blank_piece,
        )
        enc_inputs = put_row(enc_inputs, source, slot_index)
        skips = put_row(skips, result, slot_index)
        incoming = passed_along(result, "section", 1)
        return (incoming, enc_inputs, skips)

    _, enc_inputs, skips = lax.fori_loop(
        0, ticks_total, encoder_tick, (blank_piece, padded(row_shape), padded(row_shape))
    )

    def decoder_tick(tick_now, carried):
        incoming, dec_inputs, outputs = carried
        active, sample_at, slot_index = locate(tick_now, last_section - section_index)
        skip_piece = pick_row(skips, slot_index)
        source = jnp.where(section_index == last_section, skip_piece, incoming)
        joined = jnp.concatenate([source, skip_piece], axis=3)
        stamp_one = chosen_row(wide_table, sample_at)
        result = lax.cond(
            active,
            lambda: block_forward(joined, source, dec_kernel, stamp_one),
            lambda: blank_piece,
        )
        dec_inputs = put_row(dec_inputs, source, slot_index)
        outputs = put_row(outputs, result, slot_index)
        incoming = passed_along(result, "section", -1)
        return (incoming, dec_inputs, outputs)

    _, dec_inputs, outputs = lax.fori_loop(
        0, ticks_total, decoder_tick, (blank_piece, padded(row_shape), padded(row_shape))
    )

    def input_backward(inputs, weight, stamp_one, cotangent):
        activated, pullback = jax.vjp(lambda inner_field: activate(inner_field, stamp_one), inputs)
        input_grad = pullback(conv_back(cotangent, weight))[0]
        return (input_grad, activated.astype(jnp.bfloat16), cotangent.astype(jnp.bfloat16))

    top_grads = factor * (
        outputs - jnp.pad(noise.astype(jnp.float32), ((1, 1), (0, 0), (0, 0), (0, 0)))
    )

    def decoder_back_tick(tick_now, carried):
        incoming, skip_grads, up_grads, dec_acts, dec_cots = carried
        active, sample_at, slot_index = locate(tick_now, section_index)
        flowing = jnp.where(section_index == 0, pick_row(top_grads, slot_index), incoming)
        joined = jnp.concatenate(
            [pick_row(dec_inputs, slot_index), pick_row(skips, slot_index)], axis=3
        )
        stamp_one = chosen_row(wide_table, sample_at)

        def decoder_working():
            input_grad, acts, cots = input_backward(joined, dec_back_kernel, stamp_one, flowing)
            up_piece = input_grad[..., :channels] + flowing
            return (up_piece, input_grad[..., channels:], acts, cots)

        def decoder_resting():
            return (
                blank_piece,
                blank_piece,
                jnp.zeros((1,) + wide_shape, jnp.bfloat16),
                jnp.zeros((1,) + row_shape, jnp.bfloat16),
            )

        up_piece, skip_grad, acts, cots = lax.cond(active, decoder_working, decoder_resting)
        skip_grads = put_row(skip_grads, skip_grad, slot_index)
        up_grads = put_row(up_grads, up_piece, slot_index)
        dec_acts = put_row(dec_acts, acts, slot_index)
        dec_cots = put_row(dec_cots, cots, slot_index)
        incoming = passed_along(up_piece, "section", 1)
        return (incoming, skip_grads, up_grads, dec_acts, dec_cots)

    _, skip_grads, up_grads, dec_acts, dec_cots = lax.fori_loop(
        0,
        ticks_total,
        decoder_back_tick,
        (
            blank_piece,
            padded(row_shape),
            padded(row_shape),
            padded(wide_shape, jnp.bfloat16),
            padded(row_shape, jnp.bfloat16),
        ),
    )
    dec_acc = conv_weight_grad(real_rows(dec_acts), real_rows(dec_cots))

    def encoder_back_tick(tick_now, carried):
        incoming, enc_acts, enc_cots = carried
        active, sample_at, slot_index = locate(tick_now, last_section - section_index)
        arriving = jnp.where(
            section_index == last_section, pick_row(up_grads, slot_index), incoming
        )
        merged = arriving + pick_row(skip_grads, slot_index)
        block_input = pick_row(enc_inputs, slot_index)
        stamp_one = chosen_row(narrow_table, sample_at)

        def encoder_working():
            input_grad, acts, cots = input_backward(block_input, enc_back_kernel, stamp_one, merged)
            return (input_grad + merged, acts, cots)

        def encoder_resting():
            blank_half = jnp.zeros((1,) + row_shape, jnp.bfloat16)
            return (blank_piece, blank_half, blank_half)

        down_piece, acts, cots = lax.cond(active, encoder_working, encoder_resting)
        enc_acts = put_row(enc_acts, acts, slot_index)
        enc_cots = put_row(enc_cots, cots, slot_index)
        incoming = passed_along(down_piece, "section", -1)
        return (incoming, enc_acts, enc_cots)

    _, enc_acts, enc_cots = lax.fori_loop(
        0,
        ticks_total,
        encoder_back_tick,
        (blank_piece, padded(row_shape, jnp.bfloat16), padded(row_shape, jnp.bfloat16)),
    )
    enc_acc = conv_weight_grad(real_rows(enc_acts), real_rows(enc_cots))
    replicas = lax.axis_size("dp")
    enc_rows = enc_acc.shape[2] // replicas
    dec_rows = dec_acc.shape[2] // replicas
    both = jnp.concatenate(
        [
            enc_acc.reshape(3, 3, replicas, enc_rows, -1),
            dec_acc.reshape(3, 3, replicas, dec_rows, -1),
        ],
        axis=3,
    ).reshape(1, 3, 3, replicas * (enc_rows + dec_rows), -1)
    share = lax.psum_scatter(both, "dp", scatter_dimension=3, tiled=True)
    enc_share = share[:, :, :, :enc_rows]
    dec_share = share[:, :, :, enc_rows:]
    return (enc_share, dec_share)


def solution(mesh):
    placed = (
        P("dp", None, None, None),
        P("dp", None, None, None),
        P("dp"),
        P("section", None, None, None, None),
        P("section", None, None, None, None),
    )
    return jax.shard_map(
        shards,
        mesh=mesh,
        in_specs=placed,
        out_specs=(P("section", None, None, "dp", None), P("section", None, None, "dp", None)),
        check_vma=False,
    )
```

```python
import math

import jax
import jax.numpy as jnp
from jax import lax
from jax.sharding import PartitionSpec as P

GROUPS = 32


def passed_along(value, axis, steps):
    count = lax.axis_size(axis)
    initial, last = (max(0, -steps), min(count, count - steps))
    return lax.ppermute(value, axis, [(source, source + steps) for source in range(initial, last)])


def embed(stamps_in, channels):
    half_width = channels // 2
    frequency = jnp.exp(-math.log(10000.0) * jnp.arange(half_width, dtype=jnp.float32) / half_width)
    angles = stamps_in.astype(jnp.float32)[:, None] * frequency[None, :]
    return jnp.concatenate([jnp.sin(angles), jnp.cos(angles)], axis=1)


def activate(inputs_f32, modulate_row):
    batch_rows, height, breadth, channels = inputs_f32.shape
    grouped = inputs_f32.reshape(batch_rows, height * breadth, GROUPS, channels // GROUPS)
    group_mean = jnp.mean(grouped, axis=(1, 3), keepdims=True)
    centered = grouped - group_mean
    group_var = jnp.mean(centered * centered, axis=(1, 3), keepdims=True)
    normed = (centered * lax.rsqrt(group_var + 1e-05)).reshape(inputs_f32.shape)
    return jax.nn.silu(normed * modulate_row[:, None, None, :])


def conv_apply(activations, weight):
    return lax.conv_general_dilated(
        activations,
        weight,
        window_strides=(1, 1),
        padding=((1, 1), (1, 1)),
        dimension_numbers=("NHWC", "HWIO", "NHWC"),
        preferred_element_type=jnp.float32,
    )


def flipped(weight):
    return jnp.flip(weight, (0, 1)).swapaxes(2, 3)


def conv_back(cotangent, flipped_weight):
    return conv_apply(cotangent.astype(jnp.bfloat16), flipped_weight)


def conv_weight_grad(activations, cotangent):
    batch_rows, height, breadth, channels = activations.shape
    padded = jnp.pad(activations, ((0, 0), (1, 1), (1, 1), (0, 0)))
    flat_cot = cotangent.astype(jnp.bfloat16).reshape(-1, cotangent.shape[3])
    kernel_rows = []
    for row_off in range(3):
        kernel_cols = []
        for col_off in range(3):
            window = padded[:, row_off : row_off + height, col_off : col_off + breadth, :].reshape(
                -1, channels
            )
            kernel_cols.append(
                lax.dot_general(
                    window, flat_cot, (((0,), (0,)), ((), ())), preferred_element_type=jnp.float32
                )
            )
        kernel_rows.append(jnp.stack(kernel_cols))
    return jnp.stack(kernel_rows)


def modulation(stamps_in, channels):
    return 1.0 + 0.5 * embed(stamps_in, channels)


def chosen_row(table, sample_at):
    hit = (jnp.arange(table.shape[0]) == sample_at)[:, None]
    return jnp.sum(jnp.where(hit, table, 0.0), axis=0, keepdims=True)


def block_forward(inputs, residual, weight, modulate_row):
    activations = activate(inputs, modulate_row).astype(jnp.bfloat16)
    return residual + conv_apply(activations, weight)


def noise_levels(stamps_in):
    phase = (stamps_in.astype(jnp.float32) / 1000.0 + 0.008) / 1.008 * (math.pi / 2.0)
    signal = jnp.cos(phase) ** 2
    return (jnp.sqrt(signal), jnp.sqrt(1.0 - signal))


def pick_row(buffer, slot_index):
    return lax.dynamic_slice_in_dim(buffer, slot_index, 1, 0)


def put_row(buffer, piece, slot_index):
    return lax.dynamic_update_slice_in_dim(buffer, piece.astype(buffer.dtype), slot_index, 0)


def shards(clean, noise, stamps, enc_weight, dec_weight):
    sections = lax.axis_size("section")
    section_index = lax.axis_index("section")
    last_section = sections - 1
    samples = clean.shape[0]
    channels = clean.shape[3]
    enc_kernel = enc_weight[0]
    dec_kernel = dec_weight[0]
    narrow_table = modulation(stamps, channels)
    wide_table = modulation(stamps, 2 * channels)
    enc_back_kernel = flipped(enc_kernel)
    dec_back_kernel = flipped(dec_kernel)
    keep_level, spread_level = noise_levels(stamps)
    noisy = keep_level[:, None, None, None] * clean.astype(jnp.float32) + spread_level[
        :, None, None, None
    ] * noise.astype(jnp.float32)
    factor = 1.0 / math.sqrt(samples * lax.axis_size("dp") * clean.shape[1] * clean.shape[2])
    ticks_total = samples + sections - 1
    blank_piece = jnp.zeros((1,) + clean.shape[1:], jnp.float32)

    def locate(tick_now, offset):
        sample_id = tick_now - offset
        active = (sample_id >= 0) & (sample_id < samples)
        slot_index = jnp.clip(sample_id, -1, samples) + 1
        return (active, jnp.clip(sample_id, 0, samples - 1), slot_index)

    def padded(inner_shape, dtype=jnp.float32):
        return jnp.zeros((samples + 2,) + inner_shape, dtype)

    def real_rows(buffer):
        return buffer[1 : samples + 1]

    row_shape = clean.shape[1:]
    wide_shape = row_shape[:-1] + (2 * channels,)

    def encoder_tick(tick_now, carried):
        incoming, enc_inputs, skips = carried
        active, sample_at, slot_index = locate(tick_now, section_index)
        source = jnp.where(section_index == 0, pick_row(noisy, sample_at), incoming)
        stamp_one = chosen_row(narrow_table, sample_at)
        result = lax.cond(
            active,
            lambda: block_forward(source, source, enc_kernel, stamp_one),
            lambda: blank_piece,
        )
        enc_inputs = put_row(enc_inputs, source, slot_index)
        skips = put_row(skips, result, slot_index)
        incoming = passed_along(result, "section", 1)
        return (incoming, enc_inputs, skips)

    _, enc_inputs, skips = lax.fori_loop(
        0, ticks_total, encoder_tick, (blank_piece, padded(row_shape), padded(row_shape))
    )

    def decoder_tick(tick_now, carried):
        incoming, dec_inputs, outputs = carried
        active, sample_at, slot_index = locate(tick_now, last_section - section_index)
        skip_piece = pick_row(skips, slot_index)
        source = jnp.where(section_index == last_section, skip_piece, incoming)
        joined = jnp.concatenate([source, skip_piece], axis=3)
        stamp_one = chosen_row(wide_table, sample_at)
        result = lax.cond(
            active,
            lambda: block_forward(joined, source, dec_kernel, stamp_one),
            lambda: blank_piece,
        )
        dec_inputs = put_row(dec_inputs, source, slot_index)
        outputs = put_row(outputs, result, slot_index)
        incoming = passed_along(result, "section", -1)
        return (incoming, dec_inputs, outputs)

    _, dec_inputs, outputs = lax.fori_loop(
        0, ticks_total, decoder_tick, (blank_piece, padded(row_shape), padded(row_shape))
    )

    def input_backward(inputs, weight, stamp_one, cotangent):
        activated, pullback = jax.vjp(lambda inner_field: activate(inner_field, stamp_one), inputs)
        input_grad = pullback(conv_back(cotangent, weight))[0]
        return (input_grad, activated.astype(jnp.bfloat16), cotangent.astype(jnp.bfloat16))

    top_grads = factor * (
        outputs - jnp.pad(noise.astype(jnp.float32), ((1, 1), (0, 0), (0, 0), (0, 0)))
    )

    def decoder_back_tick(tick_now, carried):
        incoming, skip_grads, up_grads, dec_acts, dec_cots = carried
        active, sample_at, slot_index = locate(tick_now, section_index)
        flowing = jnp.where(section_index == 0, pick_row(top_grads, slot_index), incoming)
        joined = jnp.concatenate(
            [pick_row(dec_inputs, slot_index), pick_row(skips, slot_index)], axis=3
        )
        stamp_one = chosen_row(wide_table, sample_at)

        def decoder_working():
            input_grad, acts, cots = input_backward(joined, dec_back_kernel, stamp_one, flowing)
            up_piece = input_grad[..., :channels] + flowing
            return (up_piece, input_grad[..., channels:], acts, cots)

        def decoder_resting():
            return (
                blank_piece,
                blank_piece,
                jnp.zeros((1,) + wide_shape, jnp.bfloat16),
                jnp.zeros((1,) + row_shape, jnp.bfloat16),
            )

        up_piece, skip_grad, acts, cots = lax.cond(active, decoder_working, decoder_resting)
        skip_grads = put_row(skip_grads, skip_grad, slot_index)
        up_grads = put_row(up_grads, up_piece, slot_index)
        dec_acts = put_row(dec_acts, acts, slot_index)
        dec_cots = put_row(dec_cots, cots, slot_index)
        incoming = passed_along(up_piece, "section", 1)
        return (incoming, skip_grads, up_grads, dec_acts, dec_cots)

    _, skip_grads, up_grads, dec_acts, dec_cots = lax.fori_loop(
        0,
        ticks_total,
        decoder_back_tick,
        (
            blank_piece,
            padded(row_shape),
            padded(row_shape),
            padded(wide_shape, jnp.bfloat16),
            padded(row_shape, jnp.bfloat16),
        ),
    )
    dec_acc = conv_weight_grad(real_rows(dec_acts), real_rows(dec_cots))

    def encoder_back_tick(tick_now, carried):
        incoming, enc_acts, enc_cots = carried
        active, sample_at, slot_index = locate(tick_now, last_section - section_index)
        arriving = jnp.where(
            section_index == last_section, pick_row(up_grads, slot_index), incoming
        )
        merged = arriving + pick_row(skip_grads, slot_index)
        block_input = pick_row(enc_inputs, slot_index)
        stamp_one = chosen_row(narrow_table, sample_at)

        def encoder_working():
            input_grad, acts, cots = input_backward(block_input, enc_back_kernel, stamp_one, merged)
            return (input_grad + merged, acts, cots)

        def encoder_resting():
            blank_half = jnp.zeros((1,) + row_shape, jnp.bfloat16)
            return (blank_piece, blank_half, blank_half)

        down_piece, acts, cots = lax.cond(active, encoder_working, encoder_resting)
        enc_acts = put_row(enc_acts, acts, slot_index)
        enc_cots = put_row(enc_cots, cots, slot_index)
        incoming = passed_along(down_piece, "section", -1)
        return (incoming, enc_acts, enc_cots)

    _, enc_acts, enc_cots = lax.fori_loop(
        0,
        ticks_total,
        encoder_back_tick,
        (blank_piece, padded(row_shape, jnp.bfloat16), padded(row_shape, jnp.bfloat16)),
    )
    enc_acc = conv_weight_grad(real_rows(enc_acts), real_rows(enc_cots))
    replicas = lax.axis_size("dp")
    enc_rows = enc_acc.shape[2] // replicas
    dec_rows = dec_acc.shape[2] // replicas
    both = jnp.concatenate(
        [
            enc_acc.reshape(3, 3, replicas, enc_rows, -1),
            dec_acc.reshape(3, 3, replicas, dec_rows, -1),
        ],
        axis=3,
    ).reshape(1, 3, 3, replicas * (enc_rows + dec_rows), -1)
    share = lax.psum_scatter(both, "dp", scatter_dimension=3, tiled=True)
    enc_share = share[:, :, :, :enc_rows]
    dec_share = share[:, :, :, enc_rows:]
    return (enc_share, dec_share)


def solution(mesh):
    placed = (
        P("dp", None, None, None),
        P("dp", None, None, None),
        P("dp"),
        P("section", None, None, None, None),
        P("section", None, None, None, None),
    )
    return jax.shard_map(
        shards,
        mesh=mesh,
        in_specs=placed,
        out_specs=(P("section", None, None, "dp", None), P("section", None, None, "dp", None)),
        check_vma=False,
    )
```

```python
import math

import jax
import jax.numpy as jnp
from jax import lax
from jax.sharding import PartitionSpec as P

GROUPS = 32


def passed_along(value, axis, steps):
    count = lax.axis_size(axis)
    initial, last = (max(0, -steps), min(count, count - steps))
    pairs = [(source, source + steps) for source in range(initial, last)]
    half = value.shape[1] // 2
    pieces = [value[:, :half], value[:, half:]]
    return jnp.concatenate([lax.ppermute(piece, axis, pairs) for piece in pieces], axis=1)


def embed(stamps_in, channels):
    half_width = channels // 2
    frequency = jnp.exp(-math.log(10000.0) * jnp.arange(half_width, dtype=jnp.float32) / half_width)
    angles = stamps_in.astype(jnp.float32)[:, None] * frequency[None, :]
    return jnp.concatenate([jnp.sin(angles), jnp.cos(angles)], axis=1)


def activate(inputs_f32, modulate_row):
    batch_rows, height, breadth, channels = inputs_f32.shape
    grouped = inputs_f32.reshape(batch_rows, height * breadth, GROUPS, channels // GROUPS)
    group_mean = jnp.mean(grouped, axis=(1, 3), keepdims=True)
    centered = grouped - group_mean
    group_var = jnp.mean(centered * centered, axis=(1, 3), keepdims=True)
    normed = (centered * lax.rsqrt(group_var + 1e-05)).reshape(inputs_f32.shape)
    return jax.nn.silu(normed * modulate_row[:, None, None, :])


def conv_apply(activations, weight):
    return lax.conv_general_dilated(
        activations,
        weight,
        window_strides=(1, 1),
        padding=((1, 1), (1, 1)),
        dimension_numbers=("NHWC", "HWIO", "NHWC"),
        preferred_element_type=jnp.float32,
    )


def flipped(weight):
    return jnp.flip(weight, (0, 1)).swapaxes(2, 3)


def conv_back(cotangent, flipped_weight):
    return conv_apply(cotangent.astype(jnp.bfloat16), flipped_weight)


def conv_weight_grad(activations, cotangent):
    batch_rows, height, breadth, channels = activations.shape
    padded = jnp.pad(activations, ((0, 0), (1, 1), (1, 1), (0, 0)))
    flat_cot = cotangent.astype(jnp.bfloat16).reshape(-1, cotangent.shape[3])
    kernel_rows = []
    for row_off in range(3):
        kernel_cols = []
        for col_off in range(3):
            window = padded[:, row_off : row_off + height, col_off : col_off + breadth, :].reshape(
                -1, channels
            )
            kernel_cols.append(
                lax.dot_general(
                    window, flat_cot, (((0,), (0,)), ((), ())), preferred_element_type=jnp.float32
                )
            )
        kernel_rows.append(jnp.stack(kernel_cols))
    return jnp.stack(kernel_rows)


def modulation(stamps_in, channels):
    return 1.0 + 0.5 * embed(stamps_in, channels)


def chosen_row(table, sample_at):
    hit = (jnp.arange(table.shape[0]) == sample_at)[:, None]
    return jnp.sum(jnp.where(hit, table, 0.0), axis=0, keepdims=True)


def block_forward(inputs, residual, weight, modulate_row):
    activations = activate(inputs, modulate_row).astype(jnp.bfloat16)
    return residual + conv_apply(activations, weight)


def noise_levels(stamps_in):
    phase = (stamps_in.astype(jnp.float32) / 1000.0 + 0.008) / 1.008 * (math.pi / 2.0)
    signal = jnp.cos(phase) ** 2
    return (jnp.sqrt(signal), jnp.sqrt(1.0 - signal))


def pick_row(buffer, slot_index):
    return lax.dynamic_slice_in_dim(buffer, slot_index, 1, 0)


def put_row(buffer, piece, slot_index):
    return lax.dynamic_update_slice_in_dim(buffer, piece.astype(buffer.dtype), slot_index, 0)


def shards(clean, noise, stamps, enc_weight, dec_weight):
    sections = lax.axis_size("section")
    section_index = lax.axis_index("section")
    last_section = sections - 1
    samples = clean.shape[0]
    channels = clean.shape[3]
    enc_kernel = enc_weight[0]
    dec_kernel = dec_weight[0]
    narrow_table = modulation(stamps, channels)
    wide_table = modulation(stamps, 2 * channels)
    enc_back_kernel = flipped(enc_kernel)
    dec_back_kernel = flipped(dec_kernel)
    keep_level, spread_level = noise_levels(stamps)
    noisy = keep_level[:, None, None, None] * clean.astype(jnp.float32) + spread_level[
        :, None, None, None
    ] * noise.astype(jnp.float32)
    factor = 1.0 / math.sqrt(samples * lax.axis_size("dp") * clean.shape[1] * clean.shape[2])
    ticks_total = samples + sections - 1
    blank_piece = jnp.zeros((1,) + clean.shape[1:], jnp.float32)

    def locate(tick_now, offset):
        sample_id = tick_now - offset
        active = (sample_id >= 0) & (sample_id < samples)
        slot_index = jnp.clip(sample_id, -1, samples) + 1
        return (active, jnp.clip(sample_id, 0, samples - 1), slot_index)

    def padded(inner_shape, dtype=jnp.float32):
        return jnp.zeros((samples + 2,) + inner_shape, dtype)

    def real_rows(buffer):
        return buffer[1 : samples + 1]

    row_shape = clean.shape[1:]
    wide_shape = row_shape[:-1] + (2 * channels,)

    def encoder_tick(tick_now, carried):
        incoming, enc_inputs, skips = carried
        active, sample_at, slot_index = locate(tick_now, section_index)
        source = jnp.where(section_index == 0, pick_row(noisy, sample_at), incoming)
        stamp_one = chosen_row(narrow_table, sample_at)
        result = lax.cond(
            active,
            lambda: block_forward(source, source, enc_kernel, stamp_one),
            lambda: blank_piece,
        )
        enc_inputs = put_row(enc_inputs, source, slot_index)
        skips = put_row(skips, result, slot_index)
        incoming = passed_along(result, "section", 1)
        return (incoming, enc_inputs, skips)

    _, enc_inputs, skips = lax.fori_loop(
        0, ticks_total, encoder_tick, (blank_piece, padded(row_shape), padded(row_shape))
    )

    def decoder_tick(tick_now, carried):
        incoming, dec_inputs, outputs = carried
        active, sample_at, slot_index = locate(tick_now, last_section - section_index)
        skip_piece = pick_row(skips, slot_index)
        source = jnp.where(section_index == last_section, skip_piece, incoming)
        joined = jnp.concatenate([source, skip_piece], axis=3)
        stamp_one = chosen_row(wide_table, sample_at)
        result = lax.cond(
            active,
            lambda: block_forward(joined, source, dec_kernel, stamp_one),
            lambda: blank_piece,
        )
        dec_inputs = put_row(dec_inputs, source, slot_index)
        outputs = put_row(outputs, result, slot_index)
        incoming = passed_along(result, "section", -1)
        return (incoming, dec_inputs, outputs)

    _, dec_inputs, outputs = lax.fori_loop(
        0, ticks_total, decoder_tick, (blank_piece, padded(row_shape), padded(row_shape))
    )

    def input_backward(inputs, weight, stamp_one, cotangent):
        activated, pullback = jax.vjp(lambda inner_field: activate(inner_field, stamp_one), inputs)
        input_grad = pullback(conv_back(cotangent, weight))[0]
        return (input_grad, activated.astype(jnp.bfloat16), cotangent.astype(jnp.bfloat16))

    def decoder_back_tick(tick_now, carried):
        incoming, skip_grads, up_grads, dec_acts, dec_cots = carried
        active, sample_at, slot_index = locate(tick_now, section_index)
        top_grad = factor * (
            pick_row(outputs, slot_index) - pick_row(noise, sample_at).astype(jnp.float32)
        )
        flowing = jnp.where(section_index == 0, top_grad, incoming)
        joined = jnp.concatenate(
            [pick_row(dec_inputs, slot_index), pick_row(skips, slot_index)], axis=3
        )
        stamp_one = chosen_row(wide_table, sample_at)

        def decoder_working():
            input_grad, acts, cots = input_backward(joined, dec_back_kernel, stamp_one, flowing)
            up_piece = input_grad[..., :channels] + flowing
            return (up_piece, input_grad[..., channels:], acts, cots)

        def decoder_resting():
            return (
                blank_piece,
                blank_piece,
                jnp.zeros((1,) + wide_shape, jnp.bfloat16),
                jnp.zeros((1,) + row_shape, jnp.bfloat16),
            )

        up_piece, skip_grad, acts, cots = lax.cond(active, decoder_working, decoder_resting)
        skip_grads = put_row(skip_grads, skip_grad, slot_index)
        up_grads = put_row(up_grads, up_piece, slot_index)
        dec_acts = put_row(dec_acts, acts, slot_index)
        dec_cots = put_row(dec_cots, cots, slot_index)
        incoming = passed_along(up_piece, "section", 1)
        return (incoming, skip_grads, up_grads, dec_acts, dec_cots)

    _, skip_grads, up_grads, dec_acts, dec_cots = lax.fori_loop(
        0,
        ticks_total,
        decoder_back_tick,
        (
            blank_piece,
            padded(row_shape),
            padded(row_shape),
            padded(wide_shape, jnp.bfloat16),
            padded(row_shape, jnp.bfloat16),
        ),
    )
    dec_acc = conv_weight_grad(real_rows(dec_acts), real_rows(dec_cots))

    def encoder_back_tick(tick_now, carried):
        incoming, enc_acts, enc_cots = carried
        active, sample_at, slot_index = locate(tick_now, last_section - section_index)
        arriving = jnp.where(
            section_index == last_section, pick_row(up_grads, slot_index), incoming
        )
        merged = arriving + pick_row(skip_grads, slot_index)
        block_input = pick_row(enc_inputs, slot_index)
        stamp_one = chosen_row(narrow_table, sample_at)

        def encoder_working():
            input_grad, acts, cots = input_backward(block_input, enc_back_kernel, stamp_one, merged)
            return (input_grad + merged, acts, cots)

        def encoder_resting():
            blank_half = jnp.zeros((1,) + row_shape, jnp.bfloat16)
            return (blank_piece, blank_half, blank_half)

        down_piece, acts, cots = lax.cond(active, encoder_working, encoder_resting)
        enc_acts = put_row(enc_acts, acts, slot_index)
        enc_cots = put_row(enc_cots, cots, slot_index)
        incoming = passed_along(down_piece, "section", -1)
        return (incoming, enc_acts, enc_cots)

    _, enc_acts, enc_cots = lax.fori_loop(
        0,
        ticks_total,
        encoder_back_tick,
        (blank_piece, padded(row_shape, jnp.bfloat16), padded(row_shape, jnp.bfloat16)),
    )
    enc_acc = conv_weight_grad(real_rows(enc_acts), real_rows(enc_cots))
    replicas = lax.axis_size("dp")
    enc_rows = enc_acc.shape[2] // replicas
    dec_rows = dec_acc.shape[2] // replicas
    both = jnp.concatenate(
        [
            enc_acc.reshape(3, 3, replicas, enc_rows, -1),
            dec_acc.reshape(3, 3, replicas, dec_rows, -1),
        ],
        axis=3,
    ).reshape(1, 3, 3, replicas * (enc_rows + dec_rows), -1)
    share = lax.psum_scatter(both, "dp", scatter_dimension=3, tiled=True)
    enc_share = share[:, :, :, :enc_rows]
    dec_share = share[:, :, :, enc_rows:]
    return (enc_share, dec_share)


def solution(mesh):
    placed = (
        P("dp", None, None, None),
        P("dp", None, None, None),
        P("dp"),
        P("section", None, None, None, None),
        P("section", None, None, None, None),
    )
    return jax.shard_map(
        shards,
        mesh=mesh,
        in_specs=placed,
        out_specs=(P("section", None, None, "dp", None), P("section", None, None, "dp", None)),
        check_vma=False,
    )
```

```python
import math

import jax
import jax.numpy as jnp
from jax import lax
from jax.sharding import PartitionSpec as P

GROUPS = 32


def passed_along(value, axis, steps):
    count = lax.axis_size(axis)
    initial, last = (max(0, -steps), min(count, count - steps))
    return lax.ppermute(value, axis, [(source, source + steps) for source in range(initial, last)])


def crossing_pairs(steps):
    sections = lax.axis_size("section")
    replicas = lax.axis_size("dp")
    half, flip = (sections // 2, replicas // 2)
    pairs = []
    for source in range(max(0, -steps), min(sections, sections - steps)):
        target = source + steps
        crosses = (source < half) != (target < half)
        for replica in range(replicas):
            other = (replica + flip) % replicas if crosses else replica
            pairs.append((source * replicas + replica, target * replicas + other))
    return pairs


def passed_across(value, steps):
    return lax.ppermute(value, ("section", "dp"), crossing_pairs(steps))


def embed(stamps_in, channels):
    half_width = channels // 2
    frequency = jnp.exp(-math.log(10000.0) * jnp.arange(half_width, dtype=jnp.float32) / half_width)
    angles = stamps_in.astype(jnp.float32)[:, None] * frequency[None, :]
    return jnp.concatenate([jnp.sin(angles), jnp.cos(angles)], axis=1)


def activate(inputs_f32, modulate_row):
    batch_rows, height, breadth, channels = inputs_f32.shape
    grouped = inputs_f32.reshape(batch_rows, height * breadth, GROUPS, channels // GROUPS)
    group_mean = jnp.mean(grouped, axis=(1, 3), keepdims=True)
    centered = grouped - group_mean
    group_var = jnp.mean(centered * centered, axis=(1, 3), keepdims=True)
    normed = (centered * lax.rsqrt(group_var + 1e-05)).reshape(inputs_f32.shape)
    return jax.nn.silu(normed * modulate_row[:, None, None, :])


def conv_apply(activations, weight):
    return lax.conv_general_dilated(
        activations,
        weight,
        window_strides=(1, 1),
        padding=((1, 1), (1, 1)),
        dimension_numbers=("NHWC", "HWIO", "NHWC"),
        preferred_element_type=jnp.float32,
    )


def flipped(weight):
    return jnp.flip(weight, (0, 1)).swapaxes(2, 3)


def conv_back(cotangent, flipped_weight):
    return conv_apply(cotangent.astype(jnp.bfloat16), flipped_weight)


def conv_weight_grad(activations, cotangent):
    batch_rows, height, breadth, channels = activations.shape
    padded = jnp.pad(activations, ((0, 0), (1, 1), (1, 1), (0, 0)))
    flat_cot = cotangent.astype(jnp.bfloat16).reshape(-1, cotangent.shape[3])
    kernel_rows = []
    for row_off in range(3):
        kernel_cols = []
        for col_off in range(3):
            window = padded[:, row_off : row_off + height, col_off : col_off + breadth, :].reshape(
                -1, channels
            )
            kernel_cols.append(
                lax.dot_general(
                    window, flat_cot, (((0,), (0,)), ((), ())), preferred_element_type=jnp.float32
                )
            )
        kernel_rows.append(jnp.stack(kernel_cols))
    return jnp.stack(kernel_rows)


def modulation(stamps_in, channels):
    return 1.0 + 0.5 * embed(stamps_in, channels)


def chosen_row(table, sample_at):
    hit = (jnp.arange(table.shape[0]) == sample_at)[:, None]
    return jnp.sum(jnp.where(hit, table, 0.0), axis=0, keepdims=True)


def block_forward(inputs, residual, weight, modulate_row):
    activations = activate(inputs, modulate_row).astype(jnp.bfloat16)
    return residual + conv_apply(activations, weight)


def noise_levels(stamps_in):
    phase = (stamps_in.astype(jnp.float32) / 1000.0 + 0.008) / 1.008 * (math.pi / 2.0)
    signal = jnp.cos(phase) ** 2
    return (jnp.sqrt(signal), jnp.sqrt(1.0 - signal))


def pick_row(buffer, slot_index):
    return lax.dynamic_slice_in_dim(buffer, slot_index, 1, 0)


def put_row(buffer, piece, slot_index):
    return lax.dynamic_update_slice_in_dim(buffer, piece.astype(buffer.dtype), slot_index, 0)


def shards(clean, noise, stamps, enc_weight, dec_weight):
    sections = lax.axis_size("section")
    section_index = lax.axis_index("section")
    last_section = sections - 1
    samples = clean.shape[0]
    channels = clean.shape[3]
    enc_kernel = enc_weight[0]
    dec_kernel = dec_weight[0]
    replicas = lax.axis_size("dp")
    flipped_stamps = lax.ppermute(
        stamps.astype(jnp.float32),
        "dp",
        [(replica, (replica + replicas // 2) % replicas) for replica in range(replicas)],
    )
    held_stamps = jnp.where(section_index < sections // 2, stamps.astype(jnp.float32), flipped_stamps)
    narrow_table = modulation(held_stamps, channels)
    wide_table = modulation(held_stamps, 2 * channels)
    enc_back_kernel = flipped(enc_kernel)
    dec_back_kernel = flipped(dec_kernel)
    keep_level, spread_level = noise_levels(stamps)
    noisy = keep_level[:, None, None, None] * clean.astype(jnp.float32) + spread_level[
        :, None, None, None
    ] * noise.astype(jnp.float32)
    factor = 1.0 / math.sqrt(samples * lax.axis_size("dp") * clean.shape[1] * clean.shape[2])
    ticks_total = samples + sections - 1
    blank_piece = jnp.zeros((1,) + clean.shape[1:], jnp.float32)

    def locate(tick_now, offset):
        sample_id = tick_now - offset
        active = (sample_id >= 0) & (sample_id < samples)
        slot_index = jnp.clip(sample_id, -1, samples) + 1
        return (active, jnp.clip(sample_id, 0, samples - 1), slot_index)

    def padded(inner_shape, dtype=jnp.float32):
        return jnp.zeros((samples + 2,) + inner_shape, dtype)

    def real_rows(buffer):
        return buffer[1 : samples + 1]

    row_shape = clean.shape[1:]
    wide_shape = row_shape[:-1] + (2 * channels,)

    def encoder_tick(tick_now, carried):
        incoming, enc_inputs, skips = carried
        active, sample_at, slot_index = locate(tick_now, section_index)
        source = jnp.where(section_index == 0, pick_row(noisy, sample_at), incoming)
        stamp_one = chosen_row(narrow_table, sample_at)
        result = lax.cond(
            active,
            lambda: block_forward(source, source, enc_kernel, stamp_one),
            lambda: blank_piece,
        )
        enc_inputs = put_row(enc_inputs, source, slot_index)
        skips = put_row(skips, result, slot_index)
        incoming = passed_across(result, 1)
        return (incoming, enc_inputs, skips)

    _, enc_inputs, skips = lax.fori_loop(
        0, ticks_total, encoder_tick, (blank_piece, padded(row_shape), padded(row_shape))
    )

    def decoder_tick(tick_now, carried):
        incoming, dec_inputs, outputs = carried
        active, sample_at, slot_index = locate(tick_now, last_section - section_index)
        skip_piece = pick_row(skips, slot_index)
        source = jnp.where(section_index == last_section, skip_piece, incoming)
        joined = jnp.concatenate([source, skip_piece], axis=3)
        stamp_one = chosen_row(wide_table, sample_at)
        result = lax.cond(
            active,
            lambda: block_forward(joined, source, dec_kernel, stamp_one),
            lambda: blank_piece,
        )
        dec_inputs = put_row(dec_inputs, joined, slot_index)
        outputs = put_row(outputs, result, slot_index)
        incoming = passed_across(result, -1)
        return (incoming, dec_inputs, outputs)

    _, dec_inputs, outputs = lax.fori_loop(
        0, ticks_total, decoder_tick, (blank_piece, padded(wide_shape), padded(row_shape))
    )

    def input_backward(inputs, weight, stamp_one, cotangent):
        activated, pullback = jax.vjp(lambda inner_field: activate(inner_field, stamp_one), inputs)
        input_grad = pullback(conv_back(cotangent, weight))[0]
        return (input_grad, activated.astype(jnp.bfloat16), cotangent.astype(jnp.bfloat16))

    def decoder_back_tick(tick_now, carried):
        incoming, skip_grads, up_grads, dec_acts, dec_cots = carried
        active, sample_at, slot_index = locate(tick_now, section_index)
        top_grad = factor * (
            pick_row(outputs, slot_index) - pick_row(noise, sample_at).astype(jnp.float32)
        )
        flowing = jnp.where(section_index == 0, top_grad, incoming)
        joined = pick_row(dec_inputs, slot_index)
        stamp_one = chosen_row(wide_table, sample_at)

        def decoder_working():
            input_grad, acts, cots = input_backward(joined, dec_back_kernel, stamp_one, flowing)
            up_piece = input_grad[..., :channels] + flowing
            return (up_piece, input_grad[..., channels:], acts, cots)

        def decoder_resting():
            return (
                blank_piece,
                blank_piece,
                jnp.zeros((1,) + wide_shape, jnp.bfloat16),
                jnp.zeros((1,) + row_shape, jnp.bfloat16),
            )

        up_piece, skip_grad, acts, cots = lax.cond(active, decoder_working, decoder_resting)
        skip_grads = put_row(skip_grads, skip_grad, slot_index)
        up_grads = put_row(up_grads, up_piece, slot_index)
        dec_acts = put_row(dec_acts, acts, slot_index)
        dec_cots = put_row(dec_cots, cots, slot_index)
        incoming = passed_across(up_piece, 1)
        return (incoming, skip_grads, up_grads, dec_acts, dec_cots)

    _, skip_grads, up_grads, dec_acts, dec_cots = lax.fori_loop(
        0,
        ticks_total,
        decoder_back_tick,
        (
            blank_piece,
            padded(row_shape),
            padded(row_shape),
            padded(wide_shape, jnp.bfloat16),
            padded(row_shape, jnp.bfloat16),
        ),
    )
    dec_acc = conv_weight_grad(real_rows(dec_acts), real_rows(dec_cots))

    def encoder_back_tick(tick_now, carried):
        incoming, enc_acts, enc_cots = carried
        active, sample_at, slot_index = locate(tick_now, last_section - section_index)
        arriving = jnp.where(
            section_index == last_section, pick_row(up_grads, slot_index), incoming
        )
        merged = arriving + pick_row(skip_grads, slot_index)
        block_input = pick_row(enc_inputs, slot_index)
        stamp_one = chosen_row(narrow_table, sample_at)

        def encoder_working():
            input_grad, acts, cots = input_backward(block_input, enc_back_kernel, stamp_one, merged)
            return (input_grad + merged, acts, cots)

        def encoder_resting():
            blank_half = jnp.zeros((1,) + row_shape, jnp.bfloat16)
            return (blank_piece, blank_half, blank_half)

        down_piece, acts, cots = lax.cond(active, encoder_working, encoder_resting)
        enc_acts = put_row(enc_acts, acts, slot_index)
        enc_cots = put_row(enc_cots, cots, slot_index)
        incoming = passed_across(down_piece, -1)
        return (incoming, enc_acts, enc_cots)

    _, enc_acts, enc_cots = lax.fori_loop(
        0,
        ticks_total,
        encoder_back_tick,
        (blank_piece, padded(row_shape, jnp.bfloat16), padded(row_shape, jnp.bfloat16)),
    )
    enc_acc = conv_weight_grad(real_rows(enc_acts), real_rows(enc_cots))
    replicas = lax.axis_size("dp")
    enc_rows = enc_acc.shape[2] // replicas
    dec_rows = dec_acc.shape[2] // replicas
    both = jnp.concatenate(
        [
            enc_acc.reshape(3, 3, replicas, enc_rows, -1),
            dec_acc.reshape(3, 3, replicas, dec_rows, -1),
        ],
        axis=3,
    ).reshape(1, 3, 3, replicas * (enc_rows + dec_rows), -1)
    share = lax.psum_scatter(both, "dp", scatter_dimension=3, tiled=True)
    enc_share = share[:, :, :, :enc_rows]
    dec_share = share[:, :, :, enc_rows:]
    return (enc_share, dec_share)


def solution(mesh):
    placed = (
        P("dp", None, None, None),
        P("dp", None, None, None),
        P("dp"),
        P("section", None, None, None, None),
        P("section", None, None, None, None),
    )
    return jax.shard_map(
        shards,
        mesh=mesh,
        in_specs=placed,
        out_specs=(P("section", None, None, "dp", None), P("section", None, None, "dp", None)),
        check_vma=False,
    )
```

```python
import math

import jax
import jax.numpy as jnp
from jax import lax
from jax.sharding import PartitionSpec as P

GROUPS = 32


def passed_along(value, axis, steps):
    count = lax.axis_size(axis)
    initial, last = (max(0, -steps), min(count, count - steps))
    return lax.ppermute(value, axis, [(source, source + steps) for source in range(initial, last)])


def crossing_pairs(steps):
    sections = lax.axis_size("section")
    replicas = lax.axis_size("dp")
    half, flip = (sections // 2, replicas // 2)
    pairs = []
    for source in range(max(0, -steps), min(sections, sections - steps)):
        target = source + steps
        crosses = (source < half) != (target < half)
        for replica in range(replicas):
            other = (replica + flip) % replicas if crosses else replica
            pairs.append((source * replicas + replica, target * replicas + other))
    return pairs


def passed_across(value, steps):
    return lax.ppermute(value, ("section", "dp"), crossing_pairs(steps))


def embed(stamps_in, channels):
    half_width = channels // 2
    frequency = jnp.exp(-math.log(10000.0) * jnp.arange(half_width, dtype=jnp.float32) / half_width)
    angles = stamps_in.astype(jnp.float32)[:, None] * frequency[None, :]
    return jnp.concatenate([jnp.sin(angles), jnp.cos(angles)], axis=1)


def activate(inputs_f32, modulate_row):
    batch_rows, height, breadth, channels = inputs_f32.shape
    grouped = inputs_f32.reshape(batch_rows, height * breadth, GROUPS, channels // GROUPS)
    group_mean = jnp.mean(grouped, axis=(1, 3), keepdims=True)
    centered = grouped - group_mean
    group_var = jnp.mean(centered * centered, axis=(1, 3), keepdims=True)
    normed = (centered * lax.rsqrt(group_var + 1e-05)).reshape(inputs_f32.shape)
    return jax.nn.silu(normed * modulate_row[:, None, None, :])


def conv_apply(activations, weight):
    return lax.conv_general_dilated(
        activations,
        weight,
        window_strides=(1, 1),
        padding=((1, 1), (1, 1)),
        dimension_numbers=("NHWC", "HWIO", "NHWC"),
        preferred_element_type=jnp.float32,
    )


def flipped(weight):
    return jnp.flip(weight, (0, 1)).swapaxes(2, 3)


def conv_back(cotangent, flipped_weight):
    return conv_apply(cotangent.astype(jnp.bfloat16), flipped_weight)


def conv_weight_grad(activations, cotangent):
    batch_rows, height, breadth, channels = activations.shape
    padded = jnp.pad(activations, ((0, 0), (1, 1), (1, 1), (0, 0)))
    flat_cot = cotangent.astype(jnp.bfloat16).reshape(-1, cotangent.shape[3])
    kernel_rows = []
    for row_off in range(3):
        kernel_cols = []
        for col_off in range(3):
            window = padded[:, row_off : row_off + height, col_off : col_off + breadth, :].reshape(
                -1, channels
            )
            kernel_cols.append(
                lax.dot_general(
                    window, flat_cot, (((0,), (0,)), ((), ())), preferred_element_type=jnp.float32
                )
            )
        kernel_rows.append(jnp.stack(kernel_cols))
    return jnp.stack(kernel_rows)


def modulation(stamps_in, channels):
    return 1.0 + 0.5 * embed(stamps_in, channels)


def chosen_row(table, sample_at):
    hit = (jnp.arange(table.shape[0]) == sample_at)[:, None]
    return jnp.sum(jnp.where(hit, table, 0.0), axis=0, keepdims=True)


def block_forward(inputs, residual, weight, modulate_row):
    activations = activate(inputs, modulate_row).astype(jnp.bfloat16)
    return residual + conv_apply(activations, weight)


def noise_levels(stamps_in):
    phase = (stamps_in.astype(jnp.float32) / 1000.0 + 0.008) / 1.008 * (math.pi / 2.0)
    signal = jnp.cos(phase) ** 2
    return (jnp.sqrt(signal), jnp.sqrt(1.0 - signal))


def pick_row(buffer, slot_index):
    return lax.dynamic_slice_in_dim(buffer, slot_index, 1, 0)


def put_row(buffer, piece, slot_index):
    return lax.dynamic_update_slice_in_dim(buffer, piece.astype(buffer.dtype), slot_index, 0)


def shards(clean, noise, stamps, enc_weight, dec_weight):
    sections = lax.axis_size("section")
    section_index = lax.axis_index("section")
    last_section = sections - 1
    samples = clean.shape[0]
    channels = clean.shape[3]
    enc_kernel = enc_weight[0]
    dec_kernel = dec_weight[0]
    replicas = lax.axis_size("dp")
    flipped_stamps = lax.ppermute(
        stamps.astype(jnp.float32),
        "dp",
        [(replica, (replica + replicas // 2) % replicas) for replica in range(replicas)],
    )
    held_stamps = jnp.where(section_index < sections // 2, stamps.astype(jnp.float32), flipped_stamps)
    narrow_table = modulation(held_stamps, channels)
    wide_table = modulation(held_stamps, 2 * channels)
    enc_back_kernel = flipped(enc_kernel)
    dec_back_kernel = flipped(dec_kernel)
    keep_level, spread_level = noise_levels(stamps)
    noisy = keep_level[:, None, None, None] * clean.astype(jnp.float32) + spread_level[
        :, None, None, None
    ] * noise.astype(jnp.float32)
    factor = 1.0 / math.sqrt(samples * lax.axis_size("dp") * clean.shape[1] * clean.shape[2])
    ticks_total = samples + sections - 1
    blank_piece = jnp.zeros((1,) + clean.shape[1:], jnp.float32)

    def locate(tick_now, offset):
        sample_id = tick_now - offset
        active = (sample_id >= 0) & (sample_id < samples)
        slot_index = jnp.clip(sample_id, -1, samples) + 1
        return (active, jnp.clip(sample_id, 0, samples - 1), slot_index)

    def padded(inner_shape, dtype=jnp.float32):
        return jnp.zeros((samples + 2,) + inner_shape, dtype)

    def real_rows(buffer):
        return buffer[1 : samples + 1]

    row_shape = clean.shape[1:]
    wide_shape = row_shape[:-1] + (2 * channels,)

    def encoder_tick(tick_now, carried):
        incoming, enc_inputs, skips = carried
        active, sample_at, slot_index = locate(tick_now, section_index)
        source = jnp.where(section_index == 0, pick_row(noisy, sample_at), incoming)
        stamp_one = chosen_row(narrow_table, sample_at)
        result = lax.cond(
            active,
            lambda: block_forward(source, source, enc_kernel, stamp_one),
            lambda: blank_piece,
        )
        enc_inputs = put_row(enc_inputs, source, slot_index)
        skips = put_row(skips, result, slot_index)
        incoming = passed_across(result, 1)
        return (incoming, enc_inputs, skips)

    _, enc_inputs, skips = lax.fori_loop(
        0, ticks_total, encoder_tick, (blank_piece, padded(row_shape), padded(row_shape))
    )

    def decoder_tick(tick_now, carried):
        incoming, dec_inputs, outputs = carried
        active, sample_at, slot_index = locate(tick_now, last_section - section_index)
        skip_piece = pick_row(skips, slot_index)
        source = jnp.where(section_index == last_section, skip_piece, incoming)
        joined = jnp.concatenate([source, skip_piece], axis=3)
        stamp_one = chosen_row(wide_table, sample_at)
        result = lax.cond(
            active,
            lambda: block_forward(joined, source, dec_kernel, stamp_one),
            lambda: blank_piece,
        )
        dec_inputs = put_row(dec_inputs, source, slot_index)
        outputs = put_row(outputs, result, slot_index)
        incoming = passed_across(result, -1)
        return (incoming, dec_inputs, outputs)

    _, dec_inputs, outputs = lax.fori_loop(
        0, ticks_total, decoder_tick, (blank_piece, padded(row_shape), padded(row_shape))
    )

    def input_backward(inputs, weight, stamp_one, cotangent):
        activated, pullback = jax.vjp(lambda inner_field: activate(inner_field, stamp_one), inputs)
        input_grad = pullback(conv_back(cotangent, weight))[0]
        return (input_grad, activated.astype(jnp.bfloat16), cotangent.astype(jnp.bfloat16))

    def decoder_back_tick(tick_now, carried):
        incoming, skip_grads, dec_acts, dec_cots = carried
        active, sample_at, slot_index = locate(tick_now, section_index)
        top_grad = factor * (
            pick_row(outputs, slot_index) - pick_row(noise, sample_at).astype(jnp.float32)
        )
        flowing = jnp.where(section_index == 0, top_grad, incoming)
        joined = jnp.concatenate(
            [pick_row(dec_inputs, slot_index), pick_row(skips, slot_index)], axis=3
        )
        stamp_one = chosen_row(wide_table, sample_at)

        def decoder_working():
            input_grad, acts, cots = input_backward(joined, dec_back_kernel, stamp_one, flowing)
            up_piece = input_grad[..., :channels] + flowing
            return (up_piece, input_grad[..., channels:], acts, cots)

        def decoder_resting():
            return (
                blank_piece,
                blank_piece,
                jnp.zeros((1,) + wide_shape, jnp.bfloat16),
                jnp.zeros((1,) + row_shape, jnp.bfloat16),
            )

        up_piece, skip_grad, acts, cots = lax.cond(active, decoder_working, decoder_resting)
        kept = jnp.where(section_index == last_section, up_piece + skip_grad, skip_grad)
        skip_grads = put_row(skip_grads, kept, slot_index)
        dec_acts = put_row(dec_acts, acts, slot_index)
        dec_cots = put_row(dec_cots, cots, slot_index)
        incoming = passed_across(up_piece, 1)
        return (incoming, skip_grads, dec_acts, dec_cots)

    _, skip_grads, dec_acts, dec_cots = lax.fori_loop(
        0,
        ticks_total,
        decoder_back_tick,
        (
            blank_piece,
            padded(row_shape),
            padded(wide_shape, jnp.bfloat16),
            padded(row_shape, jnp.bfloat16),
        ),
    )
    dec_acc = conv_weight_grad(real_rows(dec_acts), real_rows(dec_cots))

    def encoder_back_tick(tick_now, carried):
        incoming, enc_acts, enc_cots = carried
        active, sample_at, slot_index = locate(tick_now, last_section - section_index)
        skip_row = pick_row(skip_grads, slot_index)
        merged = jnp.where(section_index == last_section, skip_row, incoming + skip_row)
        block_input = pick_row(enc_inputs, slot_index)
        stamp_one = chosen_row(narrow_table, sample_at)

        def encoder_working():
            input_grad, acts, cots = input_backward(block_input, enc_back_kernel, stamp_one, merged)
            return (input_grad + merged, acts, cots)

        def encoder_resting():
            blank_half = jnp.zeros((1,) + row_shape, jnp.bfloat16)
            return (blank_piece, blank_half, blank_half)

        down_piece, acts, cots = lax.cond(active, encoder_working, encoder_resting)
        enc_acts = put_row(enc_acts, acts, slot_index)
        enc_cots = put_row(enc_cots, cots, slot_index)
        incoming = passed_across(down_piece, -1)
        return (incoming, enc_acts, enc_cots)

    _, enc_acts, enc_cots = lax.fori_loop(
        0,
        ticks_total,
        encoder_back_tick,
        (blank_piece, padded(row_shape, jnp.bfloat16), padded(row_shape, jnp.bfloat16)),
    )
    enc_acc = conv_weight_grad(real_rows(enc_acts), real_rows(enc_cots))
    replicas = lax.axis_size("dp")
    enc_rows = enc_acc.shape[2] // replicas
    dec_rows = dec_acc.shape[2] // replicas
    both = jnp.concatenate(
        [
            enc_acc.reshape(3, 3, replicas, enc_rows, -1),
            dec_acc.reshape(3, 3, replicas, dec_rows, -1),
        ],
        axis=3,
    ).reshape(1, 3, 3, replicas * (enc_rows + dec_rows), -1)
    share = lax.psum_scatter(both, "dp", scatter_dimension=3, tiled=True)
    enc_share = share[:, :, :, :enc_rows]
    dec_share = share[:, :, :, enc_rows:]
    return (enc_share, dec_share)


def solution(mesh):
    placed = (
        P("dp", None, None, None),
        P("dp", None, None, None),
        P("dp"),
        P("section", None, None, None, None),
        P("section", None, None, None, None),
    )
    return jax.shard_map(
        shards,
        mesh=mesh,
        in_specs=placed,
        out_specs=(P("section", None, None, "dp", None), P("section", None, None, "dp", None)),
        check_vma=False,
    )
```

```python
import math

import jax
import jax.numpy as jnp
from jax import lax
from jax.sharding import PartitionSpec as P

GROUPS = 32


def passed_along(value, axis, steps):
    count = lax.axis_size(axis)
    initial, last = (max(0, -steps), min(count, count - steps))
    return lax.ppermute(value, axis, [(source, source + steps) for source in range(initial, last)])


def crossing_pairs(steps):
    sections = lax.axis_size("section")
    replicas = lax.axis_size("dp")
    half, flip = (sections // 2, replicas // 2)
    pairs = []
    for source in range(max(0, -steps), min(sections, sections - steps)):
        target = source + steps
        crosses = (source < half) != (target < half)
        for replica in range(replicas):
            other = (replica + flip) % replicas if crosses else replica
            pairs.append((source * replicas + replica, target * replicas + other))
    return pairs


def passed_across(value, steps):
    return lax.ppermute(value, ("section", "dp"), crossing_pairs(steps))


def embed(stamps_in, channels):
    half_width = channels // 2
    frequency = jnp.exp(-math.log(10000.0) * jnp.arange(half_width, dtype=jnp.float32) / half_width)
    angles = stamps_in.astype(jnp.float32)[:, None] * frequency[None, :]
    return jnp.concatenate([jnp.sin(angles), jnp.cos(angles)], axis=1)


def activate(inputs_f32, modulate_row):
    batch_rows, height, breadth, channels = inputs_f32.shape
    grouped = inputs_f32.reshape(batch_rows, height * breadth, GROUPS, channels // GROUPS)
    group_mean = jnp.mean(grouped, axis=(1, 3), keepdims=True)
    centered = grouped - group_mean
    group_var = jnp.mean(centered * centered, axis=(1, 3), keepdims=True)
    normed = (centered * lax.rsqrt(group_var + 1e-05)).reshape(inputs_f32.shape)
    return jax.nn.silu(normed * modulate_row[:, None, None, :])


def conv_apply(activations, weight):
    return lax.conv_general_dilated(
        activations,
        weight,
        window_strides=(1, 1),
        padding=((1, 1), (1, 1)),
        dimension_numbers=("NHWC", "HWIO", "NHWC"),
        preferred_element_type=jnp.float32,
    )


def flipped(weight):
    return jnp.flip(weight, (0, 1)).swapaxes(2, 3)


def conv_back(cotangent, flipped_weight):
    return conv_apply(cotangent.astype(jnp.bfloat16), flipped_weight)


def conv_weight_grad(activations, cotangent):
    batch_rows, height, breadth, channels = activations.shape
    padded = jnp.pad(activations, ((0, 0), (1, 1), (1, 1), (0, 0)))
    flat_cot = cotangent.astype(jnp.bfloat16).reshape(-1, cotangent.shape[3])

    def one_tap(tap, kernel):
        row_off, col_off = (tap // 3, tap % 3)
        window = lax.dynamic_slice(
            padded, (0, row_off, col_off, 0), (batch_rows, height, breadth, channels)
        ).reshape(-1, channels)
        product = lax.dot_general(
            window, flat_cot, (((0,), (0,)), ((), ())), preferred_element_type=jnp.float32
        )
        return lax.dynamic_update_slice(kernel, product[None, None], (row_off, col_off, 0, 0))

    kernel = jnp.zeros((3, 3, channels, cotangent.shape[3]), jnp.float32)
    return lax.fori_loop(0, 9, one_tap, kernel)


def modulation(stamps_in, channels):
    return 1.0 + 0.5 * embed(stamps_in, channels)


def chosen_row(table, sample_at):
    hit = (jnp.arange(table.shape[0]) == sample_at)[:, None]
    return jnp.sum(jnp.where(hit, table, 0.0), axis=0, keepdims=True)


def block_forward(inputs, residual, weight, modulate_row):
    activations = activate(inputs, modulate_row).astype(jnp.bfloat16)
    return residual + conv_apply(activations, weight)


def noise_levels(stamps_in):
    phase = (stamps_in.astype(jnp.float32) / 1000.0 + 0.008) / 1.008 * (math.pi / 2.0)
    signal = jnp.cos(phase) ** 2
    return (jnp.sqrt(signal), jnp.sqrt(1.0 - signal))


def pick_row(buffer, slot_index):
    return lax.dynamic_slice_in_dim(buffer, slot_index, 1, 0)


def put_row(buffer, piece, slot_index):
    return lax.dynamic_update_slice_in_dim(buffer, piece.astype(buffer.dtype), slot_index, 0)


def shards(clean, noise, stamps, enc_weight, dec_weight):
    sections = lax.axis_size("section")
    section_index = lax.axis_index("section")
    last_section = sections - 1
    samples = clean.shape[0]
    channels = clean.shape[3]
    enc_kernel = enc_weight[0]
    dec_kernel = dec_weight[0]
    replicas = lax.axis_size("dp")
    flipped_stamps = lax.ppermute(
        stamps.astype(jnp.float32),
        "dp",
        [(replica, (replica + replicas // 2) % replicas) for replica in range(replicas)],
    )
    held_stamps = jnp.where(section_index < sections // 2, stamps.astype(jnp.float32), flipped_stamps)
    narrow_table = modulation(held_stamps, channels)
    wide_table = modulation(held_stamps, 2 * channels)
    enc_back_kernel = flipped(enc_kernel)
    dec_back_kernel = flipped(dec_kernel)
    keep_level, spread_level = noise_levels(stamps)
    noisy = keep_level[:, None, None, None] * clean.astype(jnp.float32) + spread_level[
        :, None, None, None
    ] * noise.astype(jnp.float32)
    factor = 1.0 / math.sqrt(samples * lax.axis_size("dp") * clean.shape[1] * clean.shape[2])
    ticks_total = samples + sections - 1
    blank_piece = jnp.zeros((1,) + clean.shape[1:], jnp.float32)

    def locate(tick_now, offset):
        sample_id = tick_now - offset
        active = (sample_id >= 0) & (sample_id < samples)
        slot_index = jnp.clip(sample_id, -1, samples) + 1
        return (active, jnp.clip(sample_id, 0, samples - 1), slot_index)

    def padded(inner_shape, dtype=jnp.float32):
        return jnp.zeros((samples + 2,) + inner_shape, dtype)

    def real_rows(buffer):
        return buffer[1 : samples + 1]

    row_shape = clean.shape[1:]
    wide_shape = row_shape[:-1] + (2 * channels,)

    def encoder_tick(tick_now, carried):
        incoming, enc_inputs, skips = carried
        active, sample_at, slot_index = locate(tick_now, section_index)
        source = jnp.where(section_index == 0, pick_row(noisy, sample_at), incoming)
        stamp_one = chosen_row(narrow_table, sample_at)
        result = lax.cond(
            active,
            lambda: block_forward(source, source, enc_kernel, stamp_one),
            lambda: blank_piece,
        )
        enc_inputs = put_row(enc_inputs, source, slot_index)
        skips = put_row(skips, result, slot_index)
        incoming = passed_across(result, 1)
        return (incoming, enc_inputs, skips)

    _, enc_inputs, skips = lax.fori_loop(
        0, ticks_total, encoder_tick, (blank_piece, padded(row_shape), padded(row_shape))
    )

    def decoder_tick(tick_now, carried):
        incoming, dec_inputs, outputs = carried
        active, sample_at, slot_index = locate(tick_now, last_section - section_index)
        skip_piece = pick_row(skips, slot_index)
        source = jnp.where(section_index == last_section, skip_piece, incoming)
        joined = jnp.concatenate([source, skip_piece], axis=3)
        stamp_one = chosen_row(wide_table, sample_at)
        result = lax.cond(
            active,
            lambda: block_forward(joined, source, dec_kernel, stamp_one),
            lambda: blank_piece,
        )
        dec_inputs = put_row(dec_inputs, source, slot_index)
        outputs = put_row(outputs, result, slot_index)
        incoming = passed_across(result, -1)
        return (incoming, dec_inputs, outputs)

    _, dec_inputs, outputs = lax.fori_loop(
        0, ticks_total, decoder_tick, (blank_piece, padded(row_shape), padded(row_shape))
    )

    def input_backward(inputs, weight, stamp_one, cotangent):
        activated, pullback = jax.vjp(lambda inner_field: activate(inner_field, stamp_one), inputs)
        input_grad = pullback(conv_back(cotangent, weight))[0]
        return (input_grad, activated.astype(jnp.bfloat16), cotangent.astype(jnp.bfloat16))

    def decoder_back_tick(tick_now, carried):
        incoming, skip_grads, up_grads, dec_acts, dec_cots = carried
        active, sample_at, slot_index = locate(tick_now, section_index)
        top_grad = factor * (
            pick_row(outputs, slot_index) - pick_row(noise, sample_at).astype(jnp.float32)
        )
        flowing = jnp.where(section_index == 0, top_grad, incoming)
        joined = jnp.concatenate(
            [pick_row(dec_inputs, slot_index), pick_row(skips, slot_index)], axis=3
        )
        stamp_one = chosen_row(wide_table, sample_at)

        def decoder_working():
            input_grad, acts, cots = input_backward(joined, dec_back_kernel, stamp_one, flowing)
            up_piece = input_grad[..., :channels] + flowing
            return (up_piece, input_grad[..., channels:], acts, cots)

        def decoder_resting():
            return (
                blank_piece,
                blank_piece,
                jnp.zeros((1,) + wide_shape, jnp.bfloat16),
                jnp.zeros((1,) + row_shape, jnp.bfloat16),
            )

        up_piece, skip_grad, acts, cots = lax.cond(active, decoder_working, decoder_resting)
        skip_grads = put_row(skip_grads, skip_grad, slot_index)
        up_grads = put_row(up_grads, up_piece, slot_index)
        dec_acts = put_row(dec_acts, acts, slot_index)
        dec_cots = put_row(dec_cots, cots, slot_index)
        incoming = passed_across(up_piece, 1)
        return (incoming, skip_grads, up_grads, dec_acts, dec_cots)

    _, skip_grads, up_grads, dec_acts, dec_cots = lax.fori_loop(
        0,
        ticks_total,
        decoder_back_tick,
        (
            blank_piece,
            padded(row_shape),
            padded(row_shape),
            padded(wide_shape, jnp.bfloat16),
            padded(row_shape, jnp.bfloat16),
        ),
    )
    dec_acc = conv_weight_grad(real_rows(dec_acts), real_rows(dec_cots))

    def encoder_back_tick(tick_now, carried):
        incoming, enc_acts, enc_cots = carried
        active, sample_at, slot_index = locate(tick_now, last_section - section_index)
        arriving = jnp.where(
            section_index == last_section, pick_row(up_grads, slot_index), incoming
        )
        merged = arriving + pick_row(skip_grads, slot_index)
        block_input = pick_row(enc_inputs, slot_index)
        stamp_one = chosen_row(narrow_table, sample_at)

        def encoder_working():
            input_grad, acts, cots = input_backward(block_input, enc_back_kernel, stamp_one, merged)
            return (input_grad + merged, acts, cots)

        def encoder_resting():
            blank_half = jnp.zeros((1,) + row_shape, jnp.bfloat16)
            return (blank_piece, blank_half, blank_half)

        down_piece, acts, cots = lax.cond(active, encoder_working, encoder_resting)
        enc_acts = put_row(enc_acts, acts, slot_index)
        enc_cots = put_row(enc_cots, cots, slot_index)
        incoming = passed_across(down_piece, -1)
        return (incoming, enc_acts, enc_cots)

    _, enc_acts, enc_cots = lax.fori_loop(
        0,
        ticks_total,
        encoder_back_tick,
        (blank_piece, padded(row_shape, jnp.bfloat16), padded(row_shape, jnp.bfloat16)),
    )
    enc_acc = conv_weight_grad(real_rows(enc_acts), real_rows(enc_cots))
    replicas = lax.axis_size("dp")
    enc_rows = enc_acc.shape[2] // replicas
    dec_rows = dec_acc.shape[2] // replicas
    both = jnp.concatenate(
        [
            enc_acc.reshape(3, 3, replicas, enc_rows, -1),
            dec_acc.reshape(3, 3, replicas, dec_rows, -1),
        ],
        axis=3,
    ).reshape(1, 3, 3, replicas * (enc_rows + dec_rows), -1)
    share = lax.psum_scatter(both, "dp", scatter_dimension=3, tiled=True)
    enc_share = share[:, :, :, :enc_rows]
    dec_share = share[:, :, :, enc_rows:]
    return (enc_share, dec_share)


def solution(mesh):
    placed = (
        P("dp", None, None, None),
        P("dp", None, None, None),
        P("dp"),
        P("section", None, None, None, None),
        P("section", None, None, None, None),
    )
    return jax.shard_map(
        shards,
        mesh=mesh,
        in_specs=placed,
        out_specs=(P("section", None, None, "dp", None), P("section", None, None, "dp", None)),
        check_vma=False,
    )
```
